32 devices in a mesh: seq: 4 (over y, x), fsdp: 8 (over z, core).
Axes of the slice: x: 2, y: 2, z: 4, core: 2. Of those that a mesh axis runs over, the one named last changes fastest.
Arguments:
- tokens: bfloat16 [8, 1024, 2048], P('fsdp', 'seq'), may hold values from -6 to 6
- cotangent: bfloat16 [8, 1024, 2048], P('fsdp', 'seq'), may hold values from -6 to 6
- lengths: int32 [8], P('fsdp'), may hold values from 513 to 1024, as said below
- experts: int32 [8, 1024, 8], P('fsdp', 'seq'), may hold values from 0 to 15, all different within a row; in each aligned block of 256 rows (0 to 255, 256 to 511, ..., all dimensions but the last counted through in order) at most 136 rows name the same one
- attn_gain: bfloat16 [2048], P('fsdp'), may hold values from 0.25 to 1.75
- qkv_weight: bfloat16 [2048, 6144], P('fsdp'), may hold values from -0.125 to 0.125
- q_gain: bfloat16 [2048], P('fsdp'), may hold values from 0.25 to 1.75
- k_gain: bfloat16 [2048], P('fsdp'), may hold values from 0.25 to 1.75
- out_weight: bfloat16 [2048, 2048], P('fsdp'), may hold values from -2 to 2
- moe_gain: bfloat16 [2048], P('fsdp'), may hold values from 0.25 to 1.75
- router_weight: bfloat16 [2048, 16], P('fsdp'), may hold values from -0.0625 to 0.0625
- gate_up_weight: bfloat16 [16, 2048, 2048], P('seq', 'fsdp'), may hold values from -0.125 to 0.125
- down_weight: bfloat16 [16, 1024, 2048], P('seq', 'fsdp'), may hold values from -0.75 to 0.75
Outputs:
- block_out: bfloat16 [8, 1024, 2048], P('fsdp', 'seq')
- grad_tokens: bfloat16 [8, 1024, 2048], P('fsdp', 'seq')
- grad_attn_gain: float32 [2048], P('fsdp')
- grad_qkv_weight: float32 [2048, 6144], P('fsdp')
- grad_q_gain: float32 [2048], P('fsdp')
- grad_k_gain: float32 [2048], P('fsdp')
- grad_out_weight: float32 [2048, 2048], P('fsdp')
- grad_moe_gain: float32 [2048], P('fsdp')
- grad_router_weight: float32 [2048, 16], P('fsdp')
- grad_gate_up_weight: float32 [16, 2048, 2048], P('seq', 'fsdp')
- grad_down_weight: float32 [16, 1024, 2048], P('seq', 'fsdp')
The draws below stay inside these ranges and needn't reach their ends.
Inputs may be any that keep to these rules, and one draw needn't show every extreme that they name: `lengths`: some sequence has all 1024 slots used. Each token names 8 different experts; within the 256 slots of one device no expert is named more than 136 times.
All inputs are finite; a program needn't handle non-finite values.
Results may differ from the reference program's by a relative error of at most 0.022.
Values may be sent and summed in bfloat16 or wider, within the bound.
A program may use at most 448 MiB of HBM per device.

```python
import math
from functools import partial
import jax
import jax.numpy as jnp
import numpy as np
from jax import lax

D = 2048
HEADS = 16
HEAD = 128
FF = 1024
TOP = 8
EXPERTS = 16
TOK_DEV = 256
CAP = 136
SLOTS = 1024
SEQS = 8
N_SEQ = 4


def draw_lengths(key, part):
    first_key, second_key = jax.random.split(key)
    drawn = jax.random.randint(first_key, (SEQS,), SLOTS // 2 + 1, SLOTS + 1)
    full_index = jax.random.randint(second_key, (), 0, SEQS)
    return jnp.where(jnp.arange(SEQS) == full_index, SLOTS, drawn).astype(jnp.int32)


def block_levels(own_key, shape, cuts, low, high):
    def one(dim, parts):
        heights = jax.random.uniform(jax.random.fold_in(jax.random.fold_in(own_key, 6), dim), (parts,), jnp.float32, low / len(cuts), high / len(cuts))
        return jnp.repeat(jnp.exp(heights), shape[dim] // parts).reshape((-1,) + (1,) * (len(shape) - dim - 1))

    factor_of = one(*cuts[0])
    for cut in cuts[1:]:
        factor_of = factor_of * one(*cut)
    return factor_of


def shared_out(own_key, own, number, rows, number_of, top, most, lean):
    order = jax.random.permutation(own_key, number_of)
    heavy_load, usual = portions_of(number_of, rows * top, most, lean, True), portions_of(number_of, rows * top, most, lean, False)
    places = jnp.arange(number_of)

    def named(sizes, rotation):
        used = int((sizes > 0).sum())
        fixed = max(1, used // 4)
        moved = fixed + (places - fixed + rotation * (used - fixed)) % max(1, number_of - fixed)
        return jnp.zeros((number_of,), jnp.int32).at[order[jnp.where(places < fixed, places, moved)]].set(jnp.asarray(sizes, jnp.int32))

    sizes = jnp.where(number % 4 == 0, named(heavy_load, number // 4), named(usual, number - number // 4 - 1))
    mixed = jax.random.permutation(jax.random.fold_in(own, 3), number_of)
    source_of, sink = mixed[0:number_of // 2 * 2:2], mixed[1:number_of // 2 * 2:2]
    room = jnp.minimum(sizes[source_of] - 1, most - sizes[sink]) // 2
    room = jnp.where((source_of == order[0]) | (sink == order[0]) | (sizes[sink] == 0), 0, jnp.maximum(room, 0))
    moved = jax.random.randint(jax.random.fold_in(own, 4), (number_of // 2,), 0, 1 << 20) % (room + 1)
    sizes = sizes.at[source_of].add(-moved).at[sink].add(moved)
    items = jnp.searchsorted(jnp.cumsum(sizes), jnp.arange(rows * top), side="right").astype(jnp.int32)
    listing = items.reshape(top, rows).T
    listing = listing[jax.random.permutation(jax.random.fold_in(own, 1), rows)]
    rotation = jax.random.randint(jax.random.fold_in(own, 2), (rows, 1), 0, top)
    return jnp.take_along_axis(listing, (jnp.arange(top)[None, :] + rotation) % top, axis=1)


def portions_of(count, total, bound, slope, full):
    weights = [(1 << 20) // math.isqrt(standing ** slope) + 1 for standing in range(1, count + 1)]
    largest = bound if full else min(bound, max(-(-total // count), total * weights[0] // sum(weights)))
    least = 1 if total - largest >= count - 1 else 0
    holding, surplus = [largest] + [least] * (count - 1), total - largest - least * (count - 1)
    while surplus > 0:
        free = [i for i in range(1, count) if holding[i] < largest] or [i for i in range(1, count) if holding[i] < bound]
        mass, left = sum([weights[i] for i in free]), surplus
        for i in free:
            extra = min(bound - holding[i], max(1, left * weights[i] // mass), surplus)
            holding[i] = holding[i] + extra
            surplus = surplus - extra
    return np.array(holding)


def normal_values(key, shape, spread, reach, cuts=(), kind=jnp.bfloat16):
    values = spread * jax.random.normal(key, shape, jnp.float32)
    if cuts:
        values = values * block_levels(key, shape, cuts, -0.22, 0.18)
    return jnp.clip(values, -reach, reach).astype(kind)


def setup_inputs(seed: int = 0) -> dict:
    seeds = jax.random.split(jax.random.key(seed), 14)
    tokens = normal_values(seeds[0], (SEQS, SLOTS, D), 1.0, 6.0, ((0, 8), (1, 4)))
    cotangent = normal_values(seeds[1], (SEQS, SLOTS, D), 1.0, 6.0, ((0, 8), (1, 4)))
    lengths = draw_lengths(jax.random.fold_in(seeds[13], 71), 0)
    experts_keys = jax.random.split(jax.random.fold_in(seeds[3], 1), SEQS * SLOTS // TOK_DEV)
    experts_turns = jax.random.permutation(jax.random.fold_in(seeds[3], 3), SEQS * SLOTS // TOK_DEV)
    experts = jax.vmap(lambda own, number: shared_out(jax.random.fold_in(seeds[3], 2), own, number, TOK_DEV, EXPERTS, TOP, CAP, 2))(experts_keys, experts_turns).reshape((SEQS, SLOTS, TOP))
    attn_gain = jnp.clip(1.0 + 0.15 * jax.random.normal(seeds[4], (D,), jnp.float32), 0.25, 1.75).astype(jnp.bfloat16)
    qkv_weight = normal_values(seeds[5], (D, 3 * D), D ** -0.5, 0.125, ((0, 8),))
    q_gain = jnp.clip(1.0 + 0.15 * jax.random.normal(seeds[6], (D,), jnp.float32), 0.25, 1.75).astype(jnp.bfloat16)
    k_gain = jnp.clip(1.0 + 0.15 * jax.random.normal(seeds[7], (D,), jnp.float32), 0.25, 1.75).astype(jnp.bfloat16)
    out_weight = normal_values(seeds[8], (D, D), (max(D // 256, 1)) ** -0.5, 2.0, ((0, 8),))
    moe_gain = jnp.clip(1.0 + 0.15 * jax.random.normal(seeds[9], (D,), jnp.float32), 0.25, 1.75).astype(jnp.bfloat16)
    router_weight = normal_values(seeds[10], (D, EXPERTS), (4 * D) ** -0.5, 0.0625, ((0, 8),))
    gate_up_weight = normal_values(seeds[11], (EXPERTS, D, 2 * FF), D ** -0.5, 0.125, ((0, 4), (1, 8)))
    down_weight = normal_values(seeds[12], (EXPERTS, FF, D), (FF // 16) ** -0.5, 0.75, ((0, 4), (1, 8)))
    return {"tokens": tokens, "cotangent": cotangent, "lengths": lengths, "experts": experts, "attn_gain": attn_gain, "qkv_weight": qkv_weight, "q_gain": q_gain, "k_gain": k_gain, "out_weight": out_weight, "moe_gain": moe_gain, "router_weight": router_weight, "gate_up_weight": gate_up_weight, "down_weight": down_weight}


EPSILON = 1e-05
ROPE_BASE = 10000.0
NEG_FILL = -1e+30

@jax.custom_vjp
def low(v):
    return lax.optimization_barrier(v.astype(jnp.bfloat16)).astype(jnp.float32)

@jax.custom_vjp
def low_back(v):
    return v

def low_keep(v):
    return (low(v), None)

def low_pass(kept, grad):
    return (grad,)

def back_keep(v):
    return (v, None)

def back_low(kept, grad):
    return (low(grad),)
low.defvjp(low_keep, low_pass)
low_back.defvjp(back_keep, back_low)

def highest(form, left, right):
    return jnp.einsum(form, left, right, precision=lax.Precision.HIGHEST)

def norm_rows(values, gain_row):
    return values * lax.rsqrt(lax.optimization_barrier(jnp.mean(values * values, axis=-1, keepdims=True)) + EPSILON) * gain_row

def rope_tables(positions):
    half_width = HEAD // 2
    frequency = ROPE_BASE ** (-(jnp.arange(half_width, dtype=jnp.float32) * 2.0 / HEAD))
    angles = positions[:, None] * frequency[None, :]
    return (jnp.concatenate([jnp.cos(angles), jnp.cos(angles)], -1), jnp.concatenate([jnp.sin(angles), jnp.sin(angles)], -1))

def rotate(values, cosine_table, sine_table):
    half_width = values.shape[-1] // 2
    turned = jnp.concatenate([-values[..., half_width:], values[..., :half_width]], -1)
    return values * cosine_table[:, None, :] + turned * sine_table[:, None, :]

def attend(pieces):
    queries, keys, values, length = pieces
    count = queries.shape[0]
    scores = low_back(highest('qhd,khd->hqk', queries, keys) * HEAD ** (-0.5))
    positions = jnp.arange(count, dtype=jnp.int32)
    allowed = (positions[None, :] <= positions[:, None]) & (positions[None, :] < length)
    scores = jnp.where(allowed[None], scores, NEG_FILL)
    row_max = lax.optimization_barrier(jnp.max(scores, axis=-1, keepdims=True))
    exp_scores = jnp.exp(scores - row_max)
    probabilities = low(exp_scores / lax.optimization_barrier(jnp.sum(exp_scores, axis=-1, keepdims=True)))
    return highest('hqk,khd->qhd', probabilities, values)

def take_rows_of(block_rows, row_index):
    return jnp.take(block_rows, row_index, axis=0)

def expert_step(rows_all, total, pieces):
    gate_up, down, take_rows, slot_rows, weight_rows = pieces
    rows = low_back(jax.vmap(take_rows_of)(rows_all, take_rows))
    gate_up_out = low_back(highest('bcd,df->bcf', rows, gate_up))
    half_width = gate_up.shape[1] // 2
    hidden = low(jax.nn.silu(gate_up_out[..., :half_width]) * gate_up_out[..., half_width:])
    result = low(low_back(highest('bcf,fd->bcd', hidden, down)))
    picked = jax.vmap(take_rows_of)(result, slot_rows)
    return (total + weight_rows[..., None] * picked, None)

def reference(tokens, cotangent, lengths, experts, attn_gain, qkv_weight, q_gain, k_gain, out_weight, moe_gain, router_weight, gate_up_weight, down_weight):
    blocks = SEQS * N_SEQ
    positions = jnp.arange(SLOTS, dtype=jnp.int32)
    valid_mask = positions[None, :] < lengths[:, None]
    keep_mask = valid_mask.astype(jnp.float32)[..., None]
    expert_ids = jnp.arange(EXPERTS, dtype=jnp.int32)
    route_hits = ((experts[..., None] == expert_ids) & valid_mask[..., None, None]).astype(jnp.int32)
    routed = lax.optimization_barrier(jnp.sum(route_hits, axis=2)).astype(jnp.int32).reshape(blocks, TOK_DEV, EXPERTS)
    before = (jnp.cumsum(routed, axis=1).astype(jnp.int32) - routed).astype(jnp.int32)
    slot_of = jnp.minimum(before, CAP - 1).astype(jnp.int32)
    slot_ids = jnp.arange(CAP, dtype=jnp.int32)
    token_ids = jnp.arange(TOK_DEV, dtype=jnp.int32)
    chosen_slot = (routed[:, None, :, :] == 1) & (before[:, None, :, :] == slot_ids[None, :, None, None])
    take_rows = lax.optimization_barrier(jnp.sum(chosen_slot.astype(jnp.int32) * token_ids[None, None, :, None], axis=2)).astype(jnp.int32)
    take_all = jnp.transpose(take_rows, (2, 0, 1))
    slot_all = jnp.transpose(slot_of, (2, 0, 1))
    hit_weights = route_hits.astype(jnp.float32)
    cosine_table, sine_table = rope_tables(positions.astype(jnp.float32))

    def forward(inputs, gain_one, qkv_full, gain_q, gain_k, out_full, gain_two, router_full, gate_up_full, down_full):
        normed = low(norm_rows(inputs, gain_one))
        projected = low_back(highest('std,de->ste', normed, qkv_full))
        queries = norm_rows(projected[..., :D], gain_q).reshape(SEQS, SLOTS, HEADS, HEAD)
        keys = norm_rows(projected[..., D:2 * D], gain_k).reshape(SEQS, SLOTS, HEADS, HEAD)
        values = low(low_back(projected[..., 2 * D:].reshape(SEQS, SLOTS, HEADS, HEAD)))
        queries = low(low_back(rotate(queries, cosine_table, sine_table)))
        keys = low(low_back(rotate(keys, cosine_table, sine_table)))
        attended = lax.map(jax.checkpoint(attend), (queries, keys, values, lengths))
        attended = low(low_back(attended.reshape(SEQS, SLOTS, D)))
        branch = low_back(highest('std,de->ste', attended, out_full)) * keep_mask
        middle = inputs + branch
        normed_two = low(norm_rows(middle, gain_two))
        logits = highest('std,de->ste', normed_two, router_full)
        chosen = jnp.take_along_axis(logits, experts, axis=-1)
        row_max = lax.optimization_barrier(jnp.max(chosen, axis=-1, keepdims=True))
        exp_chosen = jnp.exp(chosen - row_max)
        gates = exp_chosen / lax.optimization_barrier(jnp.sum(exp_chosen, axis=-1, keepdims=True))
        weight_all = lax.optimization_barrier(jnp.sum(gates[..., None] * hit_weights, axis=2)).reshape(blocks, TOK_DEV, EXPERTS)
        stepper = jax.checkpoint(partial(expert_step, normed_two.reshape(blocks, TOK_DEV, D)))
        moe_sum, _ = lax.scan(stepper, jnp.zeros((blocks, TOK_DEV, D), jnp.float32), (gate_up_full, down_full, take_all, slot_all, jnp.transpose(weight_all, (2, 0, 1))))
        return middle + moe_sum.reshape(SEQS, SLOTS, D)
    output, pullback = jax.vjp(forward, tokens.astype(jnp.float32), attn_gain.astype(jnp.float32), qkv_weight.astype(jnp.float32), q_gain.astype(jnp.float32), k_gain.astype(jnp.float32), out_weight.astype(jnp.float32), moe_gain.astype(jnp.float32), router_weight.astype(jnp.float32), gate_up_weight.astype(jnp.float32), down_weight.astype(jnp.float32))
    grad_inputs, grad_one, grad_qkv, grad_qgain, grad_kgain, grad_out, grad_two, grad_router, grad_gate_up, grad_down = pullback(cotangent.astype(jnp.float32) * keep_mask)
    return (output.astype(jnp.bfloat16), grad_inputs.astype(jnp.bfloat16), grad_one, grad_qkv, grad_qgain, grad_kgain, grad_out, grad_two, grad_router, grad_gate_up, grad_down)
```

```python
from functools import partial

import jax
import jax.numpy as jnp
from jax import lax
from jax.sharding import PartitionSpec as P

HEADS = 16
HEAD = 128
TOP = 8
CAP = 136


EPSILON = 1e-05
ROPE_BASE = 10000.0
NEG_FILL = -1e30


def round_up(count, unit):
    return -(-count // unit) * unit


def rms_scale(values):
    return lax.rsqrt(jnp.mean(values * values, axis=-1, keepdims=True) + EPSILON)


def norm_back(grad_rows, unit_rows, scale_rows, gain_row):
    scaled = grad_rows * gain_row
    inner = jnp.mean(scaled * unit_rows, axis=-1, keepdims=True)
    return (scale_rows * (scaled - unit_rows * inner), jnp.sum(grad_rows * unit_rows, axis=0))


def rope_tables(positions):
    half_width = HEAD // 2
    frequency = ROPE_BASE ** (-(jnp.arange(half_width, dtype=jnp.float32) * 2.0 / HEAD))
    angles = positions[:, None] * frequency[None, :]
    return (
        jnp.concatenate([jnp.cos(angles), jnp.cos(angles)], -1),
        jnp.concatenate([jnp.sin(angles), jnp.sin(angles)], -1),
    )


def rotate(values, cosine_table, sine_table):
    half_width = values.shape[-1] // 2
    turned = jnp.concatenate([-values[..., half_width:], values[..., :half_width]], -1)
    return values * cosine_table[:, None, :] + turned * sine_table[:, None, :]


def rotate_back(grad_rows, cosine_table, sine_table):
    half_width = grad_rows.shape[-1] // 2
    sine_part = grad_rows * sine_table[:, None, :]
    return grad_rows * cosine_table[:, None, :] + jnp.concatenate(
        [sine_part[..., half_width:], -sine_part[..., :half_width]], -1
    )


def from_peer(values, step):
    if step == 0:
        return values
    count = lax.axis_size("seq")
    return lax.ppermute(values, "seq", [(rank, rank ^ step) for rank in range(count)])


def gather_blocks(values):
    return jnp.stack([from_peer(values, step) for step in range(lax.axis_size("seq"))])


def return_blocks(blocks):
    return [from_peer(blocks[step], step) for step in range(lax.axis_size("seq"))]


def in_rank_order(parts):
    seq_rank = lax.axis_index("seq")
    buffer = jnp.zeros((len(parts),) + parts[0].shape, parts[0].dtype)
    for step, part in enumerate(parts):
        start = (seq_rank ^ step,) + (0,) * part.ndim
        buffer = lax.dynamic_update_slice(buffer, part[None], start)
    return buffer


def attend_block(heads_in, places, length, row_count, block_start):
    queries, keys, values = heads_in
    query_block = lax.dynamic_slice_in_dim(queries, block_start, row_count, 0)
    query_place = lax.dynamic_slice_in_dim(places, block_start, row_count, 0)
    scores = jnp.einsum(
        "qhd,khd->hqk", query_block, keys, preferred_element_type=jnp.float32
    ) * HEAD ** (-0.5)
    allowed = (places[None, :] <= query_place[:, None]) & (places[None, :] < length)
    scores = jnp.where(allowed[None], scores, NEG_FILL)
    row_max = jnp.max(scores, axis=-1, keepdims=True)
    exp_scores = jnp.exp(scores - row_max)
    denom_sum = jnp.sum(exp_scores, axis=-1, keepdims=True)
    probabilities = (exp_scores / denom_sum).astype(jnp.bfloat16)
    attended = jnp.einsum("hqk,khd->qhd", probabilities, values, preferred_element_type=jnp.float32)
    return (attended.astype(jnp.bfloat16), jnp.transpose((row_max + jnp.log(denom_sum))[..., 0]))


def attend_back(heads_in, grad_heads, log_sums, places, length, row_count, carried, block_start):
    queries, keys, values = heads_in
    grad_keys, grad_values = carried
    score_scale = HEAD ** (-0.5)
    query_block = lax.dynamic_slice_in_dim(queries, block_start, row_count, 0)
    query_place = lax.dynamic_slice_in_dim(places, block_start, row_count, 0)
    grad_block = lax.dynamic_slice_in_dim(grad_heads, block_start, row_count, 0)
    sums_block = jnp.transpose(lax.dynamic_slice_in_dim(log_sums, block_start, row_count, 0))[
        :, :, None
    ]
    scores = (
        jnp.einsum("qhd,khd->hqk", query_block, keys, preferred_element_type=jnp.float32)
        * score_scale
    )
    allowed = (places[None, :] <= query_place[:, None]) & (places[None, :] < length)
    probabilities = jnp.where(allowed[None], jnp.exp(scores - sums_block), 0.0)
    low_probs = probabilities.astype(jnp.bfloat16)
    grad_probs = jnp.einsum("qhd,khd->hqk", grad_block, values, preferred_element_type=jnp.float32)
    grad_values = grad_values + jnp.einsum(
        "hqk,qhd->khd", low_probs, grad_block, preferred_element_type=jnp.float32
    )
    inner = jnp.sum(probabilities * grad_probs, axis=-1, keepdims=True)
    grad_scores = (probabilities * (grad_probs - inner)).astype(jnp.bfloat16)
    grad_query = (
        jnp.einsum("hqk,khd->qhd", grad_scores, keys, preferred_element_type=jnp.float32)
        * score_scale
    )
    grad_keys = (
        grad_keys
        + jnp.einsum("hqk,qhd->khd", grad_scores, query_block, preferred_element_type=jnp.float32)
        * score_scale
    )
    return ((grad_keys, grad_values), grad_query)


def mixed_dot(form, left, right):
    return jnp.einsum(form, left, right, preferred_element_type=jnp.float32)


def expert_pass(rows, grad_result_rows, slot_weight, gate_up, down):
    half_width = down.shape[0]
    gate_up_out = mixed_dot("rd,df->rf", rows, gate_up)
    gate_part = gate_up_out[:, :half_width]
    up_part = gate_up_out[:, half_width:]
    sigmoid_gate = jax.nn.sigmoid(gate_part)
    hidden = (gate_part * sigmoid_gate * up_part).astype(jnp.bfloat16)
    result = mixed_dot("rf,fd->rd", hidden, down).astype(jnp.bfloat16)
    grad_result = (grad_result_rows.astype(jnp.float32) * slot_weight[:, None]).astype(jnp.bfloat16)
    grad_hidden = mixed_dot("rd,fd->rf", grad_result, down)
    grad_gate = grad_hidden * up_part * sigmoid_gate * (1.0 + gate_part * (1.0 - sigmoid_gate))
    grad_up = grad_hidden * gate_part * sigmoid_gate
    grad_mixed = jnp.concatenate([grad_gate, grad_up], -1).astype(jnp.bfloat16)
    grad_gate_up = mixed_dot("rd,rf->df", rows, grad_mixed).astype(jnp.bfloat16)
    grad_down = mixed_dot("rf,rd->fd", hidden, grad_result).astype(jnp.bfloat16)
    grad_rows = mixed_dot("rf,df->rd", grad_mixed, gate_up).astype(jnp.bfloat16)
    grad_slot = jnp.sum(
        result.astype(jnp.float32) * grad_result_rows.astype(jnp.float32), axis=-1
    )
    weighted = (result.astype(jnp.float32) * slot_weight[:, None]).astype(jnp.bfloat16)
    return (weighted, grad_slot, grad_rows, grad_gate_up, grad_down)


def sum_small(rows):
    fsdp_count = lax.axis_size("fsdp")
    pieces = rows.reshape(rows.shape[0], fsdp_count, -1)
    pieces = lax.all_to_all(pieces, "fsdp", split_axis=1, concat_axis=1, tiled=True)
    return jnp.sum(lax.all_gather(jnp.sum(pieces, axis=1), "seq", axis=0), axis=0)


def local(
    tokens,
    cotangent,
    lengths,
    experts,
    attn_gain,
    qkv_weight,
    q_gain,
    k_gain,
    out_weight,
    moe_gain,
    router_weight,
    gate_up_weight,
    down_weight,
):
    bf16, f32 = jnp.bfloat16, jnp.float32
    seq_count = lax.axis_size("seq")
    seq_rank = lax.axis_index("seq")
    own_tokens = tokens[0]
    tok_count, model_width = own_tokens.shape
    local_count = gate_up_weight.shape[0]
    experts_count = local_count * seq_count
    own_width = model_width // seq_count
    own_heads = own_width // HEAD
    key_span = seq_count * tok_count
    length = lengths[0]
    block_ranks = seq_rank ^ jnp.arange(seq_count, dtype=jnp.int32)
    places = (
        block_ranks[:, None] * tok_count + jnp.arange(tok_count, dtype=jnp.int32)[None, :]
    ).reshape(-1)
    valid_all = (places < length).reshape(seq_count, tok_count)
    keep_mask = valid_all[0].astype(f32)[:, None]

    own_qkv = lax.dynamic_index_in_dim(
        qkv_weight.reshape(-1, 3, seq_count, own_width), seq_rank, 2, False
    ).reshape(-1, 3 * own_width)
    qkv_own = lax.all_gather(own_qkv, "fsdp", axis=0, tiled=True)
    token_blocks = gather_blocks(own_tokens)
    small_rows = jnp.concatenate(
        [jnp.stack([attn_gain, q_gain, k_gain, moe_gain]), router_weight.T], axis=0
    )
    small_full = lax.all_gather(small_rows, "fsdp", axis=1, tiled=True)
    gain_one, gain_q, gain_k, gain_two = [small_full[i].astype(f32) for i in range(4)]
    router_rows = small_full[4:]
    gain_q = lax.dynamic_slice_in_dim(gain_q, seq_rank * own_width, own_width, 0)
    gain_k = lax.dynamic_slice_in_dim(gain_k, seq_rank * own_width, own_width, 0)
    out_cut = lax.dynamic_slice_in_dim(out_weight, seq_rank * own_width, own_width, 1)
    out_cut = lax.all_gather(out_cut, "fsdp", axis=0, tiled=True)
    out_full = in_rank_order([from_peer(out_cut, step) for step in range(seq_count)])
    weights = []
    for index in range(local_count):
        weights.append(
            (
                lax.all_gather(gate_up_weight[index], "fsdp", axis=0, tiled=True),
                lax.all_gather(down_weight[index], "fsdp", axis=0, tiled=True),
            )
        )
    id_blocks = gather_blocks(experts[0])
    cot_blocks = gather_blocks(cotangent[0])

    inputs_all = token_blocks.reshape(key_span, model_width).astype(f32)
    normed = (inputs_all * rms_scale(inputs_all) * gain_one).astype(bf16)
    projected = mixed_dot("td,de->te", normed, qkv_own)
    query_raw = projected[:, :own_width]
    key_raw = projected[:, own_width : 2 * own_width]
    value_raw = projected[:, 2 * own_width :]
    squares = jnp.stack([jnp.sum(query_raw * query_raw, -1), jnp.sum(key_raw * key_raw, -1)])

    def over_heads(parts):
        blocks = parts.reshape(2, seq_count, tok_count)
        total = blocks
        for step in range(1, seq_count):
            order = jnp.array([block ^ step for block in range(seq_count)])
            total = total + from_peer(blocks, step)[:, order]
        return total.reshape(2, key_span)

    scales = lax.rsqrt(over_heads(squares) / model_width + EPSILON)[:, :, None]
    unit_q = query_raw * scales[0]
    unit_k = key_raw * scales[1]
    cosine_table, sine_table = rope_tables(places.astype(f32))
    head_shape = (key_span, own_heads, HEAD)
    query_rot = rotate((unit_q * gain_q).reshape(head_shape), cosine_table, sine_table)
    key_rot = rotate((unit_k * gain_k).reshape(head_shape), cosine_table, sine_table)
    heads_in = (
        query_rot.astype(bf16),
        key_rot.astype(bf16),
        value_raw.reshape(head_shape).astype(bf16),
    )
    row_count = min(512, key_span)
    block_starts = jnp.arange(key_span // row_count, dtype=jnp.int32) * row_count
    attended_blocks, sums_blocks = lax.map(
        partial(attend_block, heads_in, places, length, row_count), block_starts
    )
    log_sums = sums_blocks.reshape(key_span, own_heads)
    attended_parts = return_blocks(attended_blocks.reshape(seq_count, tok_count, own_width))
    attended = jnp.transpose(in_rank_order(attended_parts), (1, 0, 2))

    inputs = own_tokens.astype(f32)
    branch = mixed_dot(
        "td,jdc->tjc", attended.reshape(tok_count, model_width), out_full
    ).reshape(tok_count, model_width)
    middle = inputs + branch * keep_mask
    scale_two = rms_scale(middle)
    unit_two = middle * scale_two
    normed_two = (unit_two * gain_two).astype(bf16)

    row_blocks = gather_blocks(normed_two)
    logits = mixed_dot("btd,ed->bte", row_blocks, router_rows)
    expert_range = jnp.arange(experts_count, dtype=jnp.int32)
    named = jnp.any(id_blocks[..., None] == expert_range, axis=2)
    chosen = jnp.where(named, logits, NEG_FILL)
    exp_chosen = jnp.where(named, jnp.exp(chosen - jnp.max(chosen, -1, keepdims=True)), 0.0)
    gates = exp_chosen / jnp.sum(exp_chosen, axis=-1, keepdims=True)
    routed = (named & valid_all[..., None]).astype(jnp.int32)
    before = jnp.cumsum(routed, axis=1) - routed
    local_routed = lax.dynamic_slice_in_dim(routed, seq_rank * local_count, local_count, 2)
    local_before = lax.dynamic_slice_in_dim(before, seq_rank * local_count, local_count, 2)
    local_gates = lax.dynamic_slice_in_dim(gates, seq_rank * local_count, local_count, 2)
    slots = round_up(CAP, 16)
    slot_place = jnp.where(local_routed == 1, local_before, -1)
    slot_place = jnp.transpose(slot_place, (2, 0, 1))
    local_gates = jnp.transpose(local_gates, (2, 0, 1))
    slot_hit = slot_place[:, :, None, :] == jnp.arange(slots, dtype=jnp.int32)[:, None]
    slot_pick = slot_hit.astype(bf16)
    slot_gates = jnp.sum(jnp.where(slot_hit, local_gates[:, :, None, :], 0.0), axis=-1)

    weighted_rows, grad_row_sets, grad_slots, gate_up_sums, down_sums = [], [], [], [], []
    for index in range(local_count):
        pick = slot_pick[index]
        rows = mixed_dot("bct,btd->bcd", pick, row_blocks).astype(bf16)
        grad_source = mixed_dot("bct,btd->bcd", pick, cot_blocks).astype(bf16)
        weighted, grad_slot, grad_rows, grad_gate_up, grad_down = expert_pass(
            rows.reshape(seq_count * slots, model_width),
            grad_source.reshape(seq_count * slots, model_width),
            slot_gates[index].reshape(-1),
            *weights[index],
        )
        weighted_rows.append(weighted.reshape(seq_count, slots, model_width))
        grad_row_sets.append(grad_rows.reshape(seq_count, slots, model_width))
        grad_slots.append(
            jnp.sum(
                jnp.where(slot_hit[index], grad_slot.reshape(seq_count, slots)[:, :, None], 0.0), 1
            )
        )
        gate_up_sums.append(lax.psum_scatter(grad_gate_up, "fsdp", scatter_dimension=0, tiled=True))
        down_sums.append(lax.psum_scatter(grad_down, "fsdp", scatter_dimension=0, tiled=True))
    pick_all = jnp.concatenate([slot_pick[index] for index in range(local_count)], axis=1)
    grad_partial = mixed_dot("bct,bcd->btd", pick_all, jnp.concatenate(grad_row_sets, axis=1))
    grad_back = return_blocks(grad_partial.astype(bf16))
    grad_gates = in_rank_order(return_blocks(jnp.stack(grad_slots, axis=1)))
    moe_partial = mixed_dot("bct,bcd->btd", pick_all, jnp.concatenate(weighted_rows, axis=1))
    moe_parts = return_blocks(moe_partial.astype(bf16))
    moe_sum = sum(part.astype(f32) for part in moe_parts)
    block_out = (middle + moe_sum).astype(bf16)

    own_gates = gates[0]
    grad_gates = jnp.transpose(grad_gates, (2, 0, 1)).reshape(tok_count, experts_count)
    grad_logits = own_gates * (
        grad_gates - jnp.sum(own_gates * grad_gates, axis=-1, keepdims=True)
    )
    grad_out = cotangent[0].astype(f32) * keep_mask
    grad_normed_two = jnp.einsum(
        "te,ed->td", grad_logits, router_rows.astype(f32), precision=lax.Precision.HIGHEST
    ) + sum(part.astype(f32) for part in grad_back)
    grad_router = jnp.einsum(
        "te,td->ed", grad_logits, normed_two.astype(f32), precision=lax.Precision.HIGHEST
    )
    grad_middle_norm, grad_two = norm_back(grad_normed_two, unit_two, scale_two, gain_two)
    grad_middle = grad_out + grad_middle_norm
    grad_branch = (grad_middle * keep_mask).astype(bf16)
    grad_attended = mixed_dot(
        "tjc,jdc->td", grad_branch.reshape(tok_count, seq_count, own_width), out_full
    ).astype(bf16)
    grad_cut = mixed_dot("td,tc->dc", attended.reshape(tok_count, model_width), grad_branch)
    grad_cut = grad_cut.astype(bf16).reshape(model_width, seq_count, own_width)
    grad_cut = [
        from_peer(lax.dynamic_index_in_dim(grad_cut, seq_rank ^ step, 1, False), step)
        for step in range(seq_count)
    ]
    grad_cut = sum(part.astype(f32) for part in grad_cut).astype(bf16)

    cut_heads = grad_attended.reshape(tok_count, seq_count, own_width)
    grad_heads = jnp.stack(
        [
            from_peer(lax.dynamic_index_in_dim(cut_heads, seq_rank ^ step, 1, False), step)
            for step in range(seq_count)
        ]
    ).reshape(head_shape)
    zero_heads = jnp.zeros(head_shape, f32)
    (grad_keys, grad_values), grad_queries = lax.scan(
        partial(attend_back, heads_in, grad_heads, log_sums, places, length, row_count),
        (zero_heads, zero_heads),
        block_starts,
    )
    low = lambda rows: rows.reshape(head_shape).astype(bf16).astype(f32)
    grad_qn = rotate_back(low(grad_queries), cosine_table, sine_table).reshape(key_span, own_width)
    grad_kn = rotate_back(low(grad_keys), cosine_table, sine_table).reshape(key_span, own_width)
    scaled_q = grad_qn * gain_q
    scaled_k = grad_kn * gain_k
    inners = over_heads(
        jnp.stack([jnp.sum(scaled_q * unit_q, -1), jnp.sum(scaled_k * unit_k, -1)])
    )
    inners = (inners / model_width)[:, :, None]
    grad_projected = jnp.concatenate(
        [
            scales[0] * (scaled_q - unit_q * inners[0]),
            scales[1] * (scaled_k - unit_k * inners[1]),
            grad_values.reshape(key_span, own_width),
        ],
        axis=1,
    ).astype(bf16)
    grad_qkv = mixed_dot("td,te->de", normed, grad_projected).astype(bf16)
    grad_normed = mixed_dot("te,de->td", grad_projected, qkv_own).astype(bf16)
    grad_normed = sum(
        part.astype(f32)
        for part in return_blocks(grad_normed.reshape(seq_count, tok_count, model_width))
    )
    scale_one = rms_scale(inputs)
    grad_inputs_norm, grad_one = norm_back(grad_normed, inputs * scale_one, scale_one, gain_one)
    grad_tokens = (grad_middle + grad_inputs_norm).astype(bf16)

    qkv_sum = lax.psum_scatter(grad_qkv, "fsdp", scatter_dimension=0, tiled=True)
    qkv_sum = in_rank_order([from_peer(qkv_sum, step) for step in range(seq_count)])
    qkv_sum = jnp.transpose(
        qkv_sum.reshape(seq_count, -1, 3, own_width), (1, 2, 0, 3)
    ).reshape(-1, 3 * model_width)
    out_sum = lax.psum_scatter(grad_cut, "fsdp", scatter_dimension=0, tiled=True)
    out_sum = in_rank_order([from_peer(out_sum, step) for step in range(seq_count)])
    out_sum = jnp.transpose(out_sum, (1, 0, 2)).reshape(-1, model_width)
    early = sum_small(jnp.concatenate([grad_router, grad_two[None]], axis=0))
    placed = lambda row: lax.dynamic_update_slice(
        jnp.zeros((model_width,), f32), row, (seq_rank * own_width,)
    )
    late = sum_small(
        jnp.stack(
            [
                grad_one,
                placed(jnp.sum(grad_qn * unit_q, axis=0)),
                placed(jnp.sum(grad_kn * unit_k, axis=0)),
            ]
        )
    )
    return (
        block_out[None],
        grad_tokens[None],
        late[0],
        qkv_sum.astype(f32),
        late[1],
        late[2],
        out_sum.astype(f32),
        early[experts_count],
        early[:experts_count].T,
        jnp.stack(gate_up_sums).astype(f32),
        jnp.stack(down_sums).astype(f32),
    )


def solution(mesh):
    in_specs = (
        P("fsdp", "seq", None),
        P("fsdp", "seq", None),
        P("fsdp"),
        P("fsdp", "seq", None),
        P("fsdp"),
        P("fsdp", None),
        P("fsdp"),
        P("fsdp"),
        P("fsdp", None),
        P("fsdp"),
        P("fsdp", None),
        P("seq", "fsdp", None),
        P("seq", "fsdp", None),
    )
    out_specs = (
        P("fsdp", "seq", None),
        P("fsdp", "seq", None),
        P("fsdp"),
        P("fsdp", None),
        P("fsdp"),
        P("fsdp"),
        P("fsdp", None),
        P("fsdp"),
        P("fsdp", None),
        P("seq", "fsdp", None),
        P("seq", "fsdp", None),
    )
    return jax.shard_map(local, mesh=mesh, in_specs=in_specs, out_specs=out_specs, check_vma=False)
```

```python
from functools import partial

import jax
import jax.numpy as jnp
from jax import lax
from jax.sharding import PartitionSpec as P

HEADS = 16
HEAD = 128
TOP = 8
CAP = 136


EPSILON = 1e-05
ROPE_BASE = 10000.0
NEG_FILL = -1e30


def round_up(count, unit):
    return -(-count // unit) * unit


def rms_scale(values):
    return lax.rsqrt(jnp.mean(values * values, axis=-1, keepdims=True) + EPSILON)


def norm_back(grad_rows, unit_rows, scale_rows, gain_row):
    scaled = grad_rows * gain_row
    inner = jnp.mean(scaled * unit_rows, axis=-1, keepdims=True)
    return (scale_rows * (scaled - unit_rows * inner), jnp.sum(grad_rows * unit_rows, axis=0))


def rope_tables(positions):
    half_width = HEAD // 2
    frequency = ROPE_BASE ** (-(jnp.arange(half_width, dtype=jnp.float32) * 2.0 / HEAD))
    angles = positions[:, None] * frequency[None, :]
    return (
        jnp.concatenate([jnp.cos(angles), jnp.cos(angles)], -1),
        jnp.concatenate([jnp.sin(angles), jnp.sin(angles)], -1),
    )


def rotate(values, cosine_table, sine_table):
    half_width = values.shape[-1] // 2
    turned = jnp.concatenate([-values[..., half_width:], values[..., :half_width]], -1)
    return values * cosine_table[:, None, :] + turned * sine_table[:, None, :]


def rotate_back(grad_rows, cosine_table, sine_table):
    half_width = grad_rows.shape[-1] // 2
    sine_part = grad_rows * sine_table[:, None, :]
    return grad_rows * cosine_table[:, None, :] + jnp.concatenate(
        [sine_part[..., half_width:], -sine_part[..., :half_width]], -1
    )


def from_peer(values, step):
    if step == 0:
        return values
    count = lax.axis_size("seq")
    return lax.ppermute(values, "seq", [(rank, rank ^ step) for rank in range(count)])


def gather_blocks(values):
    return jnp.stack([from_peer(values, step) for step in range(lax.axis_size("seq"))])


def return_blocks(blocks):
    return [from_peer(blocks[step], step) for step in range(lax.axis_size("seq"))]


def in_rank_order(parts):
    seq_rank = lax.axis_index("seq")
    buffer = jnp.zeros((len(parts),) + parts[0].shape, parts[0].dtype)
    for step, part in enumerate(parts):
        start = (seq_rank ^ step,) + (0,) * part.ndim
        buffer = lax.dynamic_update_slice(buffer, part[None], start)
    return buffer


def attend_block(heads_in, places, length, row_count, block_start):
    queries, keys, values = heads_in
    query_block = lax.dynamic_slice_in_dim(queries, block_start, row_count, 0)
    query_place = lax.dynamic_slice_in_dim(places, block_start, row_count, 0)
    scores = jnp.einsum(
        "qhd,khd->hqk", query_block, keys, preferred_element_type=jnp.float32
    ) * HEAD ** (-0.5)
    allowed = (places[None, :] <= query_place[:, None]) & (places[None, :] < length)
    scores = jnp.where(allowed[None], scores, NEG_FILL)
    row_max = jnp.max(scores, axis=-1, keepdims=True)
    exp_scores = jnp.exp(scores - row_max)
    denom_sum = jnp.sum(exp_scores, axis=-1, keepdims=True)
    probabilities = (exp_scores / denom_sum).astype(jnp.bfloat16)
    attended = jnp.einsum("hqk,khd->qhd", probabilities, values, preferred_element_type=jnp.float32)
    return (attended.astype(jnp.bfloat16), jnp.transpose((row_max + jnp.log(denom_sum))[..., 0]))


def attend_back(heads_in, grad_heads, log_sums, places, length, row_count, carried, block_start):
    queries, keys, values = heads_in
    grad_keys, grad_values = carried
    score_scale = HEAD ** (-0.5)
    query_block = lax.dynamic_slice_in_dim(queries, block_start, row_count, 0)
    query_place = lax.dynamic_slice_in_dim(places, block_start, row_count, 0)
    grad_block = lax.dynamic_slice_in_dim(grad_heads, block_start, row_count, 0)
    sums_block = jnp.transpose(lax.dynamic_slice_in_dim(log_sums, block_start, row_count, 0))[
        :, :, None
    ]
    scores = (
        jnp.einsum("qhd,khd->hqk", query_block, keys, preferred_element_type=jnp.float32)
        * score_scale
    )
    allowed = (places[None, :] <= query_place[:, None]) & (places[None, :] < length)
    probabilities = jnp.where(allowed[None], jnp.exp(scores - sums_block), 0.0)
    low_probs = probabilities.astype(jnp.bfloat16)
    grad_probs = jnp.einsum("qhd,khd->hqk", grad_block, values, preferred_element_type=jnp.float32)
    grad_values = grad_values + jnp.einsum(
        "hqk,qhd->khd", low_probs, grad_block, preferred_element_type=jnp.float32
    )
    inner = jnp.sum(probabilities * grad_probs, axis=-1, keepdims=True)
    grad_scores = (probabilities * (grad_probs - inner)).astype(jnp.bfloat16)
    grad_query = (
        jnp.einsum("hqk,khd->qhd", grad_scores, keys, preferred_element_type=jnp.float32)
        * score_scale
    )
    grad_keys = (
        grad_keys
        + jnp.einsum("hqk,qhd->khd", grad_scores, query_block, preferred_element_type=jnp.float32)
        * score_scale
    )
    return ((grad_keys, grad_values), grad_query)


def mixed_dot(form, left, right):
    return jnp.einsum(form, left, right, preferred_element_type=jnp.float32)


def expert_forward(rows, grad_result_rows, slot_weight, gate_up, down):
    half_width = down.shape[0]
    gate_up_out = mixed_dot("rd,df->rf", rows, gate_up)
    gate_part = gate_up_out[:, :half_width]
    up_part = gate_up_out[:, half_width:]
    sigmoid_gate = jax.nn.sigmoid(gate_part)
    hidden = (gate_part * sigmoid_gate * up_part).astype(jnp.bfloat16)
    grad_result = (grad_result_rows.astype(jnp.float32) * slot_weight[:, None]).astype(jnp.bfloat16)
    grad_hidden = mixed_dot("rd,fd->rf", grad_result, down)
    grad_gate = grad_hidden * up_part * sigmoid_gate * (1.0 + gate_part * (1.0 - sigmoid_gate))
    grad_up = grad_hidden * gate_part * sigmoid_gate
    grad_mixed = jnp.concatenate([grad_gate, grad_up], -1).astype(jnp.bfloat16)
    grad_rows = mixed_dot("rd,fd->rf", grad_mixed, gate_up).astype(jnp.bfloat16)
    result = mixed_dot("rf,fd->rd", hidden, down).astype(jnp.bfloat16)
    grad_slot = jnp.sum(
        result.astype(jnp.float32) * grad_result_rows.astype(jnp.float32), axis=-1
    )
    weighted = (result.astype(jnp.float32) * slot_weight[:, None]).astype(jnp.bfloat16)
    return (weighted, grad_slot, grad_rows, (rows, grad_mixed, hidden, grad_result))


def expert_weights(kept):
    rows, grad_mixed, hidden, grad_result = kept
    grad_gate_up = mixed_dot("rd,rf->df", rows, grad_mixed).astype(jnp.bfloat16)
    grad_down = mixed_dot("rf,rd->fd", hidden, grad_result).astype(jnp.bfloat16)
    return (grad_gate_up, grad_down)


LINE = 4


def along(values, hops):
    pairs = [(2 * source + core, 2 * target + core) for source, target in hops for core in range(2)]
    return lax.ppermute(values, "fsdp", pairs)


def swap_cores(values):
    count = lax.axis_size("fsdp")
    return lax.ppermute(values, "fsdp", [(index, index ^ 1) for index in range(count)])


def place_block(buffer, block, chip, core):
    return lax.dynamic_update_slice(buffer, block[None, None], (chip, core, 0, 0))


def place_side(buffer, side, core):
    return lax.dynamic_update_slice(buffer, side[:, None], (0, core, 0, 0))


def line_gather(gate_up, down):
    index = lax.axis_index("fsdp")
    chip, core = index // 2, index % 2
    up_rows, width = gate_up.shape
    own = jnp.concatenate([gate_up, down], axis=0)
    right, left = yield (
        along(own, [(0, 1), (1, 2), (2, 3)]),
        along(own, [(3, 2), (2, 1), (1, 0)]),
    )
    right_two, left_two = yield (
        along(right, [(1, 2), (2, 3)]),
        along(left, [(2, 1), (1, 0)]),
    )
    right_three, left_three = yield (along(right_two, [(2, 3)]), along(left_two, [(1, 0)]))
    near = jnp.where(chip < 3, left, right)
    middle = jnp.where(chip < 2, left_two, right_two)
    far = jnp.where(chip == 0, left_three, jnp.where(chip == 3, right_three, right))
    near_chip = jnp.where(chip < 3, chip + 1, 2)
    far_chip = jnp.where(chip == 0, 3, jnp.where(chip == 3, 0, chip - 1))
    side = jnp.zeros((LINE,) + own.shape, own.dtype)
    for block, place in ((own, chip), (near, near_chip), (middle, (chip + 2) % 4), (far, far_chip)):
        side = lax.dynamic_update_slice(side, block[None], (place, 0, 0))
    other = yield swap_cores(side)
    sides = []
    for start, stop in ((0, up_rows), (up_rows, own.shape[0])):
        buffer = jnp.zeros((LINE, 2, stop - start, width), own.dtype)
        buffer = place_side(buffer, side[:, start:stop], core)
        buffer = place_side(buffer, other[:, start:stop], 1 - core)
        sides.append(buffer.reshape(-1, width))
    return tuple(sides)


def line_scatter(gate_up, down):
    f32 = jnp.float32
    index = lax.axis_index("fsdp")
    chip, core = index // 2, index % 2
    width = gate_up.shape[1]
    shaped = [grad.reshape(LINE, 2, -1, width) for grad in (gate_up, down)]
    up_rows = shaped[0].shape[2]

    def side(number):
        return jnp.concatenate(
            [lax.dynamic_index_in_dim(grad, number, 1, False) for grad in shaped], axis=1
        )

    got = yield swap_cores(side(1 - core))
    part = (side(core).astype(f32) + got.astype(f32)).astype(jnp.bfloat16)

    def take(place, landed=None):
        block = lax.dynamic_index_in_dim(part, place, 0, False)
        if landed is None:
            return block
        return (block.astype(f32) + landed.astype(f32)).astype(jnp.bfloat16)

    first = yield along(take(jnp.where(chip == 0, 3, 0)), [(0, 1), (3, 2)])
    outer, inner = yield (
        along(take(jnp.where(chip == 0, 2, 1)), [(0, 1), (3, 2)]),
        along(take(jnp.where(chip == 1, 3, 0), first), [(1, 2), (2, 1)]),
    )
    right, left = yield (
        along(
            take(jnp.minimum(chip + 1, 3), jnp.where(chip == 1, outer, inner)),
            [(0, 1), (1, 2), (2, 3)],
        ),
        along(
            take(jnp.maximum(chip - 1, 0), jnp.where(chip == 2, outer, inner)),
            [(3, 2), (2, 1), (1, 0)],
        ),
    )
    total = take(chip).astype(f32) + right.astype(f32) + left.astype(f32)
    return (total[:up_rows], total[up_rows:])


def whole_gather(gate_up, down):
    landed = yield tuple(
        lax.all_gather(part, "fsdp", axis=0, tiled=True) for part in (gate_up, down)
    )
    return tuple(landed)


def whole_scatter(gate_up, down):
    landed = yield tuple(
        lax.psum_scatter(part, "fsdp", scatter_dimension=0, tiled=True) for part in (gate_up, down)
    )
    return tuple(part.astype(jnp.float32) for part in landed)


class Stream:
    def __init__(self, rounds):
        self.rounds, self.result = rounds, None
        self.flight = next(rounds)

    def advance(self, landed):
        try:
            self.flight = self.rounds.send(landed)
        except StopIteration as stop:
            self.flight, self.result = (), stop.value


class Slots:
    def __init__(self):
        self.streams, self.tick = [], jnp.zeros((), jnp.float32)

    def start(self, rounds, *arrays):
        arrays = self.gate(arrays)
        self.streams.append(Stream(rounds(*arrays)))
        return self.streams[-1]

    def gate(self, arrays):
        return lax.optimization_barrier((arrays, self.tick))[0]

    def close(self, values):
        flights = [stream.flight for stream in self.streams]
        flights, values, self.tick = lax.optimization_barrier((flights, values, self.tick))
        for stream, landed in zip(self.streams, flights):
            stream.advance(landed)
        self.streams = [stream for stream in self.streams if stream.result is None]
        return values

    def finish(self, stream, values):
        while stream.result is None:
            values = self.close(values)
        return values


def local(
    tokens,
    cotangent,
    lengths,
    experts,
    attn_gain,
    qkv_weight,
    q_gain,
    k_gain,
    out_weight,
    moe_gain,
    router_weight,
    gate_up_weight,
    down_weight,
):
    bf16, f32 = jnp.bfloat16, jnp.float32
    seq_count = lax.axis_size("seq")
    seq_rank = lax.axis_index("seq")
    in_line = lax.axis_size("fsdp") == 2 * LINE
    gather_rounds = line_gather if in_line else whole_gather
    scatter_rounds = line_scatter if in_line else whole_scatter
    own_tokens = tokens[0]
    tok_count, model_width = own_tokens.shape
    local_count = gate_up_weight.shape[0]
    experts_count = local_count * seq_count
    own_width = model_width // seq_count
    own_heads = own_width // HEAD
    key_span = seq_count * tok_count
    length = lengths[0]
    block_ranks = seq_rank ^ jnp.arange(seq_count, dtype=jnp.int32)
    places = (
        block_ranks[:, None] * tok_count + jnp.arange(tok_count, dtype=jnp.int32)[None, :]
    ).reshape(-1)
    valid_all = (places < length).reshape(seq_count, tok_count)
    keep_mask = valid_all[0].astype(f32)[:, None]
    slots = Slots()
    slot_weights = lambda index: (gate_up_weight[index], down_weight[index])

    own_qkv = lax.dynamic_index_in_dim(
        qkv_weight.reshape(-1, 3, seq_count, own_width), seq_rank, 2, False
    ).reshape(-1, 3 * own_width)
    own_small = jnp.concatenate(
        [jnp.stack([attn_gain, q_gain, k_gain, moe_gain], axis=1), router_weight], axis=1
    )
    small_count = 4 + experts_count
    small_width = round_up(small_count, 128)
    own_small = jnp.pad(own_small, ((0, 0), (0, small_width - small_count)))
    front = jnp.concatenate([own_qkv, own_small], axis=1)
    front_full = lax.all_gather(front, "fsdp", axis=0, tiled=True)
    token_blocks = gather_blocks(own_tokens)
    id_blocks = gather_blocks(experts[0])
    out_cut = lax.dynamic_slice_in_dim(out_weight, seq_rank * own_width, own_width, 1)
    out_cut = lax.optimization_barrier((out_cut, front))[0]
    out_cut = lax.all_gather(out_cut, "fsdp", axis=0, tiled=True)
    front_full, token_blocks = slots.close((front_full, token_blocks))

    gathers = [slots.start(gather_rounds, *slot_weights(0))]
    cot_blocks = gather_blocks(slots.gate(cotangent[0]))
    qkv_own = front_full[:, : 3 * own_width]
    small_full = front_full[:, 3 * own_width : 3 * own_width + small_count].T
    gain_one, gain_q, gain_k, gain_two = [small_full[i].astype(f32) for i in range(4)]
    router_rows = small_full[4:]
    gain_q = lax.dynamic_slice_in_dim(gain_q, seq_rank * own_width, own_width, 0)
    gain_k = lax.dynamic_slice_in_dim(gain_k, seq_rank * own_width, own_width, 0)
    inputs_all = token_blocks.reshape(key_span, model_width).astype(f32)
    scale_all = rms_scale(inputs_all)
    normed = (inputs_all * scale_all * gain_one).astype(bf16)
    projected = mixed_dot("td,de->te", normed, qkv_own)
    query_raw = projected[:, :own_width]
    key_raw = projected[:, own_width : 2 * own_width]
    value_raw = projected[:, 2 * own_width :]
    squares = jnp.stack([jnp.sum(query_raw * query_raw, -1), jnp.sum(key_raw * key_raw, -1)])

    def over_heads(parts):
        blocks = parts.reshape(2, seq_count, tok_count)
        total = blocks
        for step in range(1, seq_count):
            order = jnp.array([block ^ step for block in range(seq_count)])
            total = total + from_peer(blocks, step)[:, order]
        return total.reshape(2, key_span)

    scales = lax.rsqrt(over_heads(squares) / model_width + EPSILON)[:, :, None]
    unit_q = query_raw * scales[0]
    unit_k = key_raw * scales[1]
    cosine_table, sine_table = rope_tables(places.astype(f32))
    head_shape = (key_span, own_heads, HEAD)
    query_rot = rotate((unit_q * gain_q).reshape(head_shape), cosine_table, sine_table)
    key_rot = rotate((unit_k * gain_k).reshape(head_shape), cosine_table, sine_table)
    heads_in = (
        query_rot.astype(bf16),
        key_rot.astype(bf16),
        value_raw.reshape(head_shape).astype(bf16),
    )
    heads_in = slots.close(heads_in)

    row_count = min(512, key_span)
    block_starts = jnp.arange(key_span // row_count, dtype=jnp.int32) * row_count
    attended_blocks, sums_blocks = lax.map(
        partial(attend_block, heads_in, places, length, row_count), block_starts
    )
    log_sums = sums_blocks.reshape(key_span, own_heads)
    out_parts = [from_peer(out_cut, step) for step in range(seq_count)]
    attended_blocks, cot_blocks, out_parts = slots.close((attended_blocks, cot_blocks, out_parts))

    out_full = in_rank_order(out_parts)
    attended_parts = return_blocks(attended_blocks.reshape(seq_count, tok_count, own_width))
    attended = jnp.transpose(in_rank_order(attended_parts), (1, 0, 2))
    inputs = own_tokens.astype(f32)
    branch = mixed_dot(
        "td,jdc->tjc", attended.reshape(tok_count, model_width), out_full
    ).reshape(tok_count, model_width)
    middle = inputs + branch * keep_mask
    scale_two = rms_scale(middle)
    unit_two = middle * scale_two
    normed_two = (unit_two * gain_two).astype(bf16)
    normed_two = slots.close(normed_two)

    gathers.append(slots.start(gather_rounds, *slot_weights(1)))
    row_blocks = slots.close(gather_blocks(normed_two))

    logits = mixed_dot("btd,ed->bte", row_blocks, router_rows)
    expert_range = jnp.arange(experts_count, dtype=jnp.int32)
    named = jnp.any(id_blocks[..., None] == expert_range, axis=2)
    chosen = jnp.where(named, logits, NEG_FILL)
    exp_chosen = jnp.where(named, jnp.exp(chosen - jnp.max(chosen, -1, keepdims=True)), 0.0)
    gates = exp_chosen / jnp.sum(exp_chosen, axis=-1, keepdims=True)
    routed = (named & valid_all[..., None]).astype(jnp.int32)
    before = jnp.cumsum(routed, axis=1) - routed
    local_routed = lax.dynamic_slice_in_dim(routed, seq_rank * local_count, local_count, 2)
    local_before = lax.dynamic_slice_in_dim(before, seq_rank * local_count, local_count, 2)
    local_gates = lax.dynamic_slice_in_dim(gates, seq_rank * local_count, local_count, 2)
    slot_count = round_up(CAP, 16)
    slot_place = jnp.where(local_routed == 1, local_before, -1)
    slot_place = jnp.transpose(slot_place, (2, 0, 1))
    local_gates = jnp.transpose(local_gates, (2, 0, 1))
    slot_hit = slot_place[:, :, None, :] == jnp.arange(slot_count, dtype=jnp.int32)[:, None]
    slot_pick = slot_hit.astype(bf16)
    slot_gates = jnp.sum(jnp.where(slot_hit, local_gates[:, :, None, :], 0.0), axis=-1)

    def picked(index):
        return tuple(
            mixed_dot("bct,btd->bcd", slot_pick[index], blocks)
            .astype(bf16)
            .reshape(seq_count * slot_count, model_width)
            for blocks in (row_blocks, cot_blocks)
        )

    def computed(index, pair):
        weighted, grad_slot, grad_rows, kept = expert_forward(
            *pair, slot_gates[index].reshape(-1), *gathers[index].result
        )
        weighted_rows.append(weighted.reshape(seq_count, slot_count, model_width))
        grad_row_sets.append(grad_rows.reshape(seq_count, slot_count, model_width))
        grad_slots.append(
            jnp.sum(
                jnp.where(
                    slot_hit[index], grad_slot.reshape(seq_count, slot_count)[:, :, None], 0.0
                ),
                1,
            )
        )
        return kept

    weighted_rows, grad_row_sets, grad_slots, scatters = [], [], [], []
    pair = slots.close(picked(0))

    for index in range(local_count):
        pair = slots.finish(gathers[index], pair)
        kept = computed(index, pair)
        last = index == local_count - 1
        if last:
            break
        grads = slots.close(expert_weights(kept))
        pair = picked(index + 1)
        if index + 2 < local_count:
            gathers.append(slots.start(gather_rounds, *slot_weights(index + 2)))
        scatters.append(slots.start(scatter_rounds, *grads))
        pair = slots.close(pair)
    pick_all = jnp.concatenate([slot_pick[index] for index in range(local_count)], axis=1)
    grad_partial = mixed_dot("bct,bcd->btd", pick_all, jnp.concatenate(grad_row_sets, axis=1))
    grad_partial, grad_slots, kept = slots.close(
        (grad_partial.astype(bf16), jnp.stack(grad_slots, axis=1), kept)
    )

    grad_back = return_blocks(grad_partial)
    grad_gates = return_blocks(grad_slots)
    moe_partial = mixed_dot("bct,bcd->btd", pick_all, jnp.concatenate(weighted_rows, axis=1))
    grads, grad_back, grad_gates, moe_partial = slots.close(
        (expert_weights(kept), grad_back, grad_gates, moe_partial.astype(bf16))
    )
    scatters.append(slots.start(scatter_rounds, *grads))

    own_gates = gates[0]
    grad_gates = jnp.transpose(in_rank_order(grad_gates), (2, 0, 1)).reshape(
        tok_count, experts_count
    )
    grad_logits = own_gates * (
        grad_gates - jnp.sum(own_gates * grad_gates, axis=-1, keepdims=True)
    )
    grad_out = cotangent[0].astype(f32) * keep_mask
    grad_normed_two = jnp.einsum(
        "te,ed->td", grad_logits, router_rows.astype(f32), precision=lax.Precision.HIGHEST
    ) + sum(part.astype(f32) for part in grad_back)
    grad_router = jnp.einsum(
        "te,td->ed", grad_logits, normed_two.astype(f32), precision=lax.Precision.HIGHEST
    )
    grad_middle_norm, grad_two = norm_back(grad_normed_two, unit_two, scale_two, gain_two)
    grad_middle = grad_out + grad_middle_norm
    grad_branch = (grad_middle * keep_mask).astype(bf16)
    grad_attended = mixed_dot(
        "tjc,jdc->td", grad_branch.reshape(tok_count, seq_count, own_width), out_full
    ).astype(bf16)
    cut_heads = grad_attended.reshape(tok_count, seq_count, own_width)
    grad_heads = jnp.stack(
        [
            from_peer(lax.dynamic_index_in_dim(cut_heads, seq_rank ^ step, 1, False), step)
            for step in range(seq_count)
        ]
    ).reshape(head_shape)
    grad_heads, grad_branch, moe_partial = slots.close((grad_heads, grad_branch, moe_partial))

    moe_parts = return_blocks(moe_partial)
    grad_cut = mixed_dot("td,tc->dc", attended.reshape(tok_count, model_width), grad_branch)
    grad_cut = grad_cut.astype(bf16).reshape(model_width, seq_count, own_width)
    grad_cut = [
        from_peer(lax.dynamic_index_in_dim(grad_cut, seq_rank ^ step, 1, False), step)
        for step in range(seq_count)
    ]
    zero_heads = jnp.zeros(head_shape, f32)
    (grad_keys, grad_values), grad_queries = lax.scan(
        partial(attend_back, heads_in, grad_heads, log_sums, places, length, row_count),
        (zero_heads, zero_heads),
        block_starts,
    )
    grad_keys, grad_values, grad_queries, grad_cut, moe_parts = slots.close(
        (grad_keys, grad_values, grad_queries, grad_cut, moe_parts)
    )

    moe_sum = sum(part.astype(f32) for part in moe_parts)
    block_out = (middle + moe_sum).astype(bf16)
    grad_cut = sum(part.astype(f32) for part in grad_cut).astype(bf16)
    low = lambda rows: rows.reshape(head_shape).astype(bf16).astype(f32)
    grad_qn = rotate_back(low(grad_queries), cosine_table, sine_table).reshape(key_span, own_width)
    grad_kn = rotate_back(low(grad_keys), cosine_table, sine_table).reshape(key_span, own_width)
    scaled_q = grad_qn * gain_q
    scaled_k = grad_kn * gain_k
    inners = over_heads(
        jnp.stack([jnp.sum(scaled_q * unit_q, -1), jnp.sum(scaled_k * unit_k, -1)])
    )
    inners = (inners / model_width)[:, :, None]
    grad_projected = jnp.concatenate(
        [
            scales[0] * (scaled_q - unit_q * inners[0]),
            scales[1] * (scaled_k - unit_k * inners[1]),
            grad_values.reshape(key_span, own_width),
        ],
        axis=1,
    ).astype(bf16)
    grad_normed = mixed_dot("te,de->td", grad_projected, qkv_own)
    grad_one = jnp.sum(grad_normed * (inputs_all * scale_all), axis=0)
    grad_qkv = mixed_dot("td,te->de", normed, grad_projected).astype(bf16)
    placed = lambda row: lax.dynamic_update_slice(
        jnp.zeros((model_width,), f32), row, (seq_rank * own_width,)
    )
    grad_small = jnp.concatenate(
        [
            jnp.stack(
                [
                    grad_one,
                    placed(jnp.sum(grad_qn * unit_q, axis=0)),
                    placed(jnp.sum(grad_kn * unit_k, axis=0)),
                    grad_two,
                ]
            ),
            grad_router,
            jnp.zeros((small_width - small_count, model_width), f32),
        ],
        axis=0,
    )
    grad_front = jnp.concatenate([grad_qkv, grad_small.T.astype(bf16)], axis=1)
    grad_front, grad_normed = slots.close((grad_front, grad_normed.astype(bf16)))

    front_sum = lax.psum_scatter(grad_front, "fsdp", scatter_dimension=0, tiled=True)
    out_sum = lax.psum_scatter(grad_cut, "fsdp", scatter_dimension=0, tiled=True)
    grad_normed = return_blocks(grad_normed.reshape(seq_count, tok_count, model_width))
    grad_normed = slots.finish(scatters[-1], grad_normed)
    grad_normed = sum(part.astype(f32) for part in grad_normed)
    scale_one = rms_scale(inputs)
    scaled = grad_normed * gain_one
    unit_one = inputs * scale_one
    inner = jnp.mean(scaled * unit_one, axis=-1, keepdims=True)
    grad_tokens = (grad_middle + scale_one * (scaled - unit_one * inner)).astype(bf16)
    front_parts = [from_peer(front_sum, step) for step in range(seq_count)]
    small_sum = sum(part[:, 3 * own_width :].astype(f32) for part in front_parts)
    qkv_sum = in_rank_order([part[:, : 3 * own_width] for part in front_parts])
    qkv_sum = jnp.transpose(
        qkv_sum.reshape(seq_count, -1, 3, own_width), (1, 2, 0, 3)
    ).reshape(-1, 3 * model_width)
    out_sum = in_rank_order([from_peer(out_sum, step) for step in range(seq_count)])
    out_sum = jnp.transpose(out_sum, (1, 0, 2)).reshape(-1, model_width)
    sums = [stream.result for stream in scatters]
    return (
        block_out[None],
        grad_tokens[None],
        small_sum[:, 0],
        qkv_sum.astype(f32),
        small_sum[:, 1],
        small_sum[:, 2],
        out_sum.astype(f32),
        small_sum[:, 3],
        small_sum[:, 4:small_count],
        jnp.stack([pair[0] for pair in sums]),
        jnp.stack([pair[1] for pair in sums]),
    )


def solution(mesh):
    in_specs = (
        P("fsdp", "seq", None),
        P("fsdp", "seq", None),
        P("fsdp"),
        P("fsdp", "seq", None),
        P("fsdp"),
        P("fsdp", None),
        P("fsdp"),
        P("fsdp"),
        P("fsdp", None),
        P("fsdp"),
        P("fsdp", None),
        P("seq", "fsdp", None),
        P("seq", "fsdp", None),
    )
    out_specs = (
        P("fsdp", "seq", None),
        P("fsdp", "seq", None),
        P("fsdp"),
        P("fsdp", None),
        P("fsdp"),
        P("fsdp"),
        P("fsdp", None),
        P("fsdp"),
        P("fsdp", None),
        P("seq", "fsdp", None),
        P("seq", "fsdp", None),
    )
    return jax.shard_map(local, mesh=mesh, in_specs=in_specs, out_specs=out_specs, check_vma=False)
```

```python
from functools import partial

import jax
import jax.numpy as jnp
from jax import lax
from jax.sharding import PartitionSpec as P

HEADS = 16
HEAD = 128
TOP = 8
CAP = 136


EPSILON = 1e-05
ROPE_BASE = 10000.0
NEG_FILL = -1e30


def round_up(count, unit):
    return -(-count // unit) * unit


def rms_scale(values):
    return lax.rsqrt(jnp.mean(values * values, axis=-1, keepdims=True) + EPSILON)


def norm_back(grad_rows, unit_rows, scale_rows, gain_row):
    scaled = grad_rows * gain_row
    inner = jnp.mean(scaled * unit_rows, axis=-1, keepdims=True)
    return (scale_rows * (scaled - unit_rows * inner), jnp.sum(grad_rows * unit_rows, axis=0))


def rope_tables(positions):
    half_width = HEAD // 2
    frequency = ROPE_BASE ** (-(jnp.arange(half_width, dtype=jnp.float32) * 2.0 / HEAD))
    angles = positions[:, None] * frequency[None, :]
    return (
        jnp.concatenate([jnp.cos(angles), jnp.cos(angles)], -1),
        jnp.concatenate([jnp.sin(angles), jnp.sin(angles)], -1),
    )


def rotate(values, cosine_table, sine_table):
    half_width = values.shape[-1] // 2
    turned = jnp.concatenate([-values[..., half_width:], values[..., :half_width]], -1)
    return values * cosine_table[:, None, :] + turned * sine_table[:, None, :]


def rotate_back(grad_rows, cosine_table, sine_table):
    half_width = grad_rows.shape[-1] // 2
    sine_part = grad_rows * sine_table[:, None, :]
    return grad_rows * cosine_table[:, None, :] + jnp.concatenate(
        [sine_part[..., half_width:], -sine_part[..., :half_width]], -1
    )


def from_peer(values, step):
    if step == 0:
        return values
    count = lax.axis_size("seq")
    return lax.ppermute(values, "seq", [(rank, rank ^ step) for rank in range(count)])


def gather_blocks(values):
    return jnp.stack([from_peer(values, step) for step in range(lax.axis_size("seq"))])


def return_blocks(blocks):
    return [from_peer(blocks[step], step) for step in range(lax.axis_size("seq"))]


def in_rank_order(parts):
    seq_rank = lax.axis_index("seq")
    buffer = jnp.zeros((len(parts),) + parts[0].shape, parts[0].dtype)
    for step, part in enumerate(parts):
        start = (seq_rank ^ step,) + (0,) * part.ndim
        buffer = lax.dynamic_update_slice(buffer, part[None], start)
    return buffer


def attend_block(heads_in, places, length, row_count, block_start):
    queries, keys, values = heads_in
    query_block = lax.dynamic_slice_in_dim(queries, block_start, row_count, 0)
    query_place = lax.dynamic_slice_in_dim(places, block_start, row_count, 0)
    scores = jnp.einsum(
        "qhd,khd->hqk", query_block, keys, preferred_element_type=jnp.float32
    ) * HEAD ** (-0.5)
    allowed = (places[None, :] <= query_place[:, None]) & (places[None, :] < length)
    scores = jnp.where(allowed[None], scores, NEG_FILL)
    row_max = jnp.max(scores, axis=-1, keepdims=True)
    exp_scores = jnp.exp(scores - row_max)
    denom_sum = jnp.sum(exp_scores, axis=-1, keepdims=True)
    probabilities = (exp_scores / denom_sum).astype(jnp.bfloat16)
    attended = jnp.einsum("hqk,khd->qhd", probabilities, values, preferred_element_type=jnp.float32)
    return (attended.astype(jnp.bfloat16), jnp.transpose((row_max + jnp.log(denom_sum))[..., 0]))


def attend_back(heads_in, grad_heads, log_sums, places, length, row_count, carried, block_start):
    queries, keys, values = heads_in
    grad_keys, grad_values = carried
    score_scale = HEAD ** (-0.5)
    query_block = lax.dynamic_slice_in_dim(queries, block_start, row_count, 0)
    query_place = lax.dynamic_slice_in_dim(places, block_start, row_count, 0)
    grad_block = lax.dynamic_slice_in_dim(grad_heads, block_start, row_count, 0)
    sums_block = jnp.transpose(lax.dynamic_slice_in_dim(log_sums, block_start, row_count, 0))[
        :, :, None
    ]
    scores = (
        jnp.einsum("qhd,khd->hqk", query_block, keys, preferred_element_type=jnp.float32)
        * score_scale
    )
    allowed = (places[None, :] <= query_place[:, None]) & (places[None, :] < length)
    probabilities = jnp.where(allowed[None], jnp.exp(scores - sums_block), 0.0)
    low_probs = probabilities.astype(jnp.bfloat16)
    grad_probs = jnp.einsum("qhd,khd->hqk", grad_block, values, preferred_element_type=jnp.float32)
    grad_values = grad_values + jnp.einsum(
        "hqk,qhd->khd", low_probs, grad_block, preferred_element_type=jnp.float32
    )
    inner = jnp.sum(probabilities * grad_probs, axis=-1, keepdims=True)
    grad_scores = (probabilities * (grad_probs - inner)).astype(jnp.bfloat16)
    grad_query = (
        jnp.einsum("hqk,khd->qhd", grad_scores, keys, preferred_element_type=jnp.float32)
        * score_scale
    )
    grad_keys = (
        grad_keys
        + jnp.einsum("hqk,qhd->khd", grad_scores, query_block, preferred_element_type=jnp.float32)
        * score_scale
    )
    return ((grad_keys, grad_values), grad_query)


def mixed_dot(form, left, right):
    return jnp.einsum(form, left, right, preferred_element_type=jnp.float32)


def expert_forward(rows, grad_result_rows, slot_weight, gate_up, down):
    half_width = down.shape[0]
    gate_up_out = mixed_dot("rd,df->rf", rows, gate_up)
    gate_part = gate_up_out[:, :half_width]
    up_part = gate_up_out[:, half_width:]
    sigmoid_gate = jax.nn.sigmoid(gate_part)
    hidden = (gate_part * sigmoid_gate * up_part).astype(jnp.bfloat16)
    grad_result = (grad_result_rows.astype(jnp.float32) * slot_weight[:, None]).astype(jnp.bfloat16)
    grad_hidden = mixed_dot("rd,fd->rf", grad_result, down)
    grad_gate = grad_hidden * up_part * sigmoid_gate * (1.0 + gate_part * (1.0 - sigmoid_gate))
    grad_up = grad_hidden * gate_part * sigmoid_gate
    grad_mixed = jnp.concatenate([grad_gate, grad_up], -1).astype(jnp.bfloat16)
    grad_rows = mixed_dot("rd,fd->rf", grad_mixed, gate_up).astype(jnp.bfloat16)
    result = mixed_dot("rf,fd->rd", hidden, down).astype(jnp.bfloat16)
    grad_slot = jnp.sum(
        result.astype(jnp.float32) * grad_result_rows.astype(jnp.float32), axis=-1
    )
    weighted = (result.astype(jnp.float32) * slot_weight[:, None]).astype(jnp.bfloat16)
    return (weighted, grad_slot, grad_rows, (rows, grad_mixed, hidden, grad_result))


def expert_weights(kept):
    rows, grad_mixed, hidden, grad_result = kept
    grad_gate_up = mixed_dot("rd,rf->df", rows, grad_mixed).astype(jnp.bfloat16)
    grad_down = mixed_dot("rf,rd->fd", hidden, grad_result).astype(jnp.bfloat16)
    return (grad_gate_up, grad_down)


def after(values, *earlier):
    return lax.optimization_barrier((values, earlier))[0]


def split_rows(stacked, up_rows):
    count = lax.axis_size("fsdp")
    width = stacked.shape[-1]
    stacked = stacked.reshape(count, -1, width)
    return (stacked[:, :up_rows].reshape(-1, width), stacked[:, up_rows:].reshape(-1, width))


def stack_rows(gate_up, down):
    count = lax.axis_size("fsdp")
    width = gate_up.shape[-1]
    parts = [grad.reshape(count, -1, width) for grad in (gate_up, down)]
    return jnp.concatenate(parts, axis=1).reshape(-1, width)


def local(
    tokens,
    cotangent,
    lengths,
    experts,
    attn_gain,
    qkv_weight,
    q_gain,
    k_gain,
    out_weight,
    moe_gain,
    router_weight,
    gate_up_weight,
    down_weight,
):
    bf16, f32 = jnp.bfloat16, jnp.float32
    seq_count = lax.axis_size("seq")
    seq_rank = lax.axis_index("seq")
    own_tokens = tokens[0]
    tok_count, model_width = own_tokens.shape
    local_count = gate_up_weight.shape[0]
    experts_count = local_count * seq_count
    own_width = model_width // seq_count
    own_heads = own_width // HEAD
    key_span = seq_count * tok_count
    length = lengths[0]
    block_ranks = seq_rank ^ jnp.arange(seq_count, dtype=jnp.int32)
    places = (
        block_ranks[:, None] * tok_count + jnp.arange(tok_count, dtype=jnp.int32)[None, :]
    ).reshape(-1)
    valid_all = (places < length).reshape(seq_count, tok_count)
    keep_mask = valid_all[0].astype(f32)[:, None]
    up_rows = gate_up_weight.shape[1]
    shards = [
        jnp.concatenate([gate_up_weight[index], down_weight[index]], axis=0)
        for index in range(local_count)
    ]

    own_qkv = lax.dynamic_index_in_dim(
        qkv_weight.reshape(-1, 3, seq_count, own_width), seq_rank, 2, False
    ).reshape(-1, 3 * own_width)
    own_small = jnp.concatenate(
        [jnp.stack([attn_gain, q_gain, k_gain, moe_gain], axis=1), router_weight], axis=1
    )
    small_count = 4 + experts_count
    small_width = round_up(small_count, 128)
    own_small = jnp.pad(own_small, ((0, 0), (0, small_width - small_count)))
    front = jnp.concatenate([own_qkv, own_small], axis=1)
    front_full = lax.all_gather(front, "fsdp", axis=0, tiled=True)
    token_blocks = gather_blocks(own_tokens)
    out_cut = lax.dynamic_slice_in_dim(out_weight, seq_rank * own_width, own_width, 1)
    out_cut = lax.all_gather(after(out_cut, front), "fsdp", axis=0, tiled=True)
    gather_expert = lambda index, *earlier: lax.all_gather(
        after(shards[index], *earlier), "fsdp", axis=0, tiled=True
    )
    weights = [gather_expert(0, front_full)]
    id_rows = experts[0].astype(bf16).reshape(-1, model_width)
    cot_parts = gather_blocks(
        after(jnp.concatenate([cotangent[0], id_rows], axis=0), token_blocks)
    )
    cot_blocks = cot_parts[:, :tok_count]
    id_blocks = cot_parts[:, tok_count:].reshape(seq_count, tok_count, -1).astype(jnp.int32)

    qkv_own = front_full[:, : 3 * own_width]
    small_full = front_full[:, 3 * own_width : 3 * own_width + small_count].T
    gain_one, gain_q, gain_k, gain_two = [small_full[i].astype(f32) for i in range(4)]
    router_rows = small_full[4:]
    gain_q = lax.dynamic_slice_in_dim(gain_q, seq_rank * own_width, own_width, 0)
    gain_k = lax.dynamic_slice_in_dim(gain_k, seq_rank * own_width, own_width, 0)
    inputs_all = token_blocks.reshape(key_span, model_width).astype(f32)
    scale_all = rms_scale(inputs_all)
    normed = (inputs_all * scale_all * gain_one).astype(bf16)
    projected = mixed_dot("td,de->te", normed, qkv_own)
    query_raw = projected[:, :own_width]
    key_raw = projected[:, own_width : 2 * own_width]
    value_raw = projected[:, 2 * own_width :]
    squares = jnp.stack([jnp.sum(query_raw * query_raw, -1), jnp.sum(key_raw * key_raw, -1)])

    def over_heads(parts):
        blocks = parts.reshape(2, seq_count, tok_count)
        total = blocks
        for step in range(1, seq_count):
            order = jnp.array([block ^ step for block in range(seq_count)])
            total = total + from_peer(blocks, step)[:, order]
        return total.reshape(2, key_span)

    scales = lax.rsqrt(over_heads(squares) / model_width + EPSILON)[:, :, None]
    unit_q = query_raw * scales[0]
    unit_k = key_raw * scales[1]
    cosine_table, sine_table = rope_tables(places.astype(f32))
    head_shape = (key_span, own_heads, HEAD)
    query_rot = rotate((unit_q * gain_q).reshape(head_shape), cosine_table, sine_table)
    key_rot = rotate((unit_k * gain_k).reshape(head_shape), cosine_table, sine_table)
    heads_in = (
        query_rot.astype(bf16),
        key_rot.astype(bf16),
        value_raw.reshape(head_shape).astype(bf16),
    )

    row_count = min(512, key_span)
    block_starts = jnp.arange(key_span // row_count, dtype=jnp.int32) * row_count
    attended_blocks, sums_blocks = lax.map(
        partial(attend_block, heads_in, places, length, row_count), block_starts
    )
    log_sums = sums_blocks.reshape(key_span, own_heads)
    weights.append(gather_expert(1, heads_in))
    out_cut = after(out_cut, heads_in)
    out_parts = [from_peer(out_cut, step) for step in range(seq_count)]

    out_full = in_rank_order(out_parts)
    attended_parts = return_blocks(attended_blocks.reshape(seq_count, tok_count, own_width))
    attended = jnp.transpose(in_rank_order(attended_parts), (1, 0, 2))
    inputs = own_tokens.astype(f32)
    branch = mixed_dot(
        "td,jdc->tjc", attended.reshape(tok_count, model_width), out_full
    ).reshape(tok_count, model_width)
    middle = inputs + branch * keep_mask
    scale_two = rms_scale(middle)
    unit_two = middle * scale_two
    normed_two = (unit_two * gain_two).astype(bf16)

    row_blocks = gather_blocks(normed_two)
    weights.append(gather_expert(2, normed_two))
    weights += [gather_expert(index, row_blocks) for index in range(3, local_count)]
    logits = mixed_dot("btd,ed->bte", row_blocks, router_rows)
    expert_range = jnp.arange(experts_count, dtype=jnp.int32)
    named = jnp.any(id_blocks[..., None] == expert_range, axis=2)
    chosen = jnp.where(named, logits, NEG_FILL)
    exp_chosen = jnp.where(named, jnp.exp(chosen - jnp.max(chosen, -1, keepdims=True)), 0.0)
    gates = exp_chosen / jnp.sum(exp_chosen, axis=-1, keepdims=True)
    routed = (named & valid_all[..., None]).astype(jnp.int32)
    before = jnp.cumsum(routed, axis=1) - routed
    local_routed = lax.dynamic_slice_in_dim(routed, seq_rank * local_count, local_count, 2)
    local_before = lax.dynamic_slice_in_dim(before, seq_rank * local_count, local_count, 2)
    local_gates = lax.dynamic_slice_in_dim(gates, seq_rank * local_count, local_count, 2)
    slot_count = round_up(CAP, 16)
    slot_place = jnp.where(local_routed == 1, local_before, -1)
    slot_place = jnp.transpose(slot_place, (2, 0, 1))
    local_gates = jnp.transpose(local_gates, (2, 0, 1))
    slot_hit = slot_place[:, :, None, :] == jnp.arange(slot_count, dtype=jnp.int32)[:, None]
    slot_pick = slot_hit.astype(bf16)
    slot_gates = jnp.sum(jnp.where(slot_hit, local_gates[:, :, None, :], 0.0), axis=-1)

    def picked(index):
        return tuple(
            mixed_dot("bct,btd->bcd", slot_pick[index], blocks)
            .astype(bf16)
            .reshape(seq_count * slot_count, model_width)
            for blocks in (row_blocks, cot_blocks)
        )

    def computed(index, pair):
        weighted, grad_slot, grad_rows, kept = expert_forward(
            *pair, slot_gates[index].reshape(-1), *split_rows(weights[index], up_rows)
        )
        weighted_rows.append(weighted.reshape(seq_count, slot_count, model_width))
        grad_row_sets.append(grad_rows.reshape(seq_count, slot_count, model_width))
        grad_slots.append(
            jnp.sum(
                jnp.where(
                    slot_hit[index], grad_slot.reshape(seq_count, slot_count)[:, :, None], 0.0
                ),
                1,
            )
        )
        return kept

    weighted_rows, grad_row_sets, grad_slots, sums = [], [], [], []
    scatter = lambda grads: lax.psum_scatter(grads, "fsdp", scatter_dimension=0, tiled=True)
    pair = picked(0)
    for index in range(local_count):
        kept = computed(index, pair)
        if index + 1 < local_count:
            grads = stack_rows(*expert_weights(kept))
            sums.append(scatter(after(grads, *sums[: max(0, index - 1)])))
            pair = after(picked(index + 1), grads)
    pick_all = jnp.concatenate([slot_pick[index] for index in range(local_count)], axis=1)
    grad_partial = mixed_dot("bct,bcd->btd", pick_all, jnp.concatenate(grad_row_sets, axis=1))

    grad_gates = return_blocks(jnp.stack(grad_slots, axis=1))
    grad_back = return_blocks(grad_partial.astype(bf16))
    moe_partial = mixed_dot("bct,bcd->btd", pick_all, jnp.concatenate(weighted_rows, axis=1))
    grads = stack_rows(*expert_weights(kept))
    grad_back = after(grad_back, grads, moe_partial.astype(bf16))

    own_gates = gates[0]
    grad_gates = jnp.transpose(in_rank_order(grad_gates), (2, 0, 1)).reshape(
        tok_count, experts_count
    )
    grad_logits = own_gates * (
        grad_gates - jnp.sum(own_gates * grad_gates, axis=-1, keepdims=True)
    )
    grad_out = cotangent[0].astype(f32) * keep_mask
    grad_normed_two = jnp.einsum(
        "te,ed->td", grad_logits, router_rows.astype(f32), precision=lax.Precision.HIGHEST
    ) + sum(part.astype(f32) for part in grad_back)
    grad_router = jnp.einsum(
        "te,td->ed", grad_logits, normed_two.astype(f32), precision=lax.Precision.HIGHEST
    )
    grad_middle_norm, grad_two = norm_back(grad_normed_two, unit_two, scale_two, gain_two)
    grad_middle = grad_out + grad_middle_norm
    grad_branch = (grad_middle * keep_mask).astype(bf16)
    grad_attended = mixed_dot(
        "tjc,jdc->td", grad_branch.reshape(tok_count, seq_count, own_width), out_full
    ).astype(bf16)
    cut_heads = grad_attended.reshape(tok_count, seq_count, own_width)
    grad_heads = jnp.stack(
        [
            from_peer(lax.dynamic_index_in_dim(cut_heads, seq_rank ^ step, 1, False), step)
            for step in range(seq_count)
        ]
    ).reshape(head_shape)

    grad_branch = after(grad_branch, grad_heads)
    grad_cut = mixed_dot("td,tc->dc", attended.reshape(tok_count, model_width), grad_branch)
    grad_cut = grad_cut.astype(bf16).reshape(model_width, seq_count, own_width)
    grad_cut = [
        from_peer(lax.dynamic_index_in_dim(grad_cut, seq_rank ^ step, 1, False), step)
        for step in range(seq_count)
    ]
    zero_heads = jnp.zeros(head_shape, f32)
    (grad_keys, grad_values), grad_queries = lax.scan(
        partial(attend_back, heads_in, grad_heads, log_sums, places, length, row_count),
        (zero_heads, zero_heads),
        block_starts,
    )

    grad_cut = sum(part.astype(f32) for part in grad_cut).astype(bf16)
    low = lambda rows: rows.reshape(head_shape).astype(bf16).astype(f32)
    grad_qn = rotate_back(low(grad_queries), cosine_table, sine_table).reshape(key_span, own_width)
    grad_kn = rotate_back(low(grad_keys), cosine_table, sine_table).reshape(key_span, own_width)
    scaled_q = grad_qn * gain_q
    scaled_k = grad_kn * gain_k
    inners = over_heads(
        jnp.stack([jnp.sum(scaled_q * unit_q, -1), jnp.sum(scaled_k * unit_k, -1)])
    )
    inners = (inners / model_width)[:, :, None]
    grad_projected = jnp.concatenate(
        [
            scales[0] * (scaled_q - unit_q * inners[0]),
            scales[1] * (scaled_k - unit_k * inners[1]),
            grad_values.reshape(key_span, own_width),
        ],
        axis=1,
    ).astype(bf16)
    grad_normed = mixed_dot("te,de->td", grad_projected, qkv_own)
    grad_one = jnp.sum(grad_normed * (inputs_all * scale_all), axis=0)
    grad_qkv = mixed_dot("td,te->de", normed, grad_projected).astype(bf16)
    placed = lambda row: lax.dynamic_update_slice(
        jnp.zeros((model_width,), f32), row, (seq_rank * own_width,)
    )
    grad_small = jnp.concatenate(
        [
            jnp.stack(
                [
                    grad_one,
                    placed(jnp.sum(grad_qn * unit_q, axis=0)),
                    placed(jnp.sum(grad_kn * unit_k, axis=0)),
                    grad_two,
                ]
            ),
            grad_router,
            jnp.zeros((small_width - small_count, model_width), f32),
        ],
        axis=0,
    )
    grad_front = jnp.concatenate([grad_qkv, grad_small.T.astype(bf16)], axis=1)

    front_sum = scatter(after(grad_front, *sums[:-1]))
    out_sum = scatter(after(grad_cut, *sums, grad_front))
    sums.append(scatter(after(grads, front_sum)))
    grad_normed = return_blocks(grad_normed.astype(bf16).reshape(seq_count, tok_count, model_width))
    moe_parts = return_blocks(after(moe_partial.astype(bf16), grad_normed))
    block_out = (middle + sum(part.astype(f32) for part in moe_parts)).astype(bf16)
    grad_normed = sum(part.astype(f32) for part in grad_normed)
    scale_one = rms_scale(inputs)
    scaled = grad_normed * gain_one
    unit_one = inputs * scale_one
    inner = jnp.mean(scaled * unit_one, axis=-1, keepdims=True)
    grad_tokens = (grad_middle + scale_one * (scaled - unit_one * inner)).astype(bf16)
    front_parts = [from_peer(front_sum, step) for step in range(seq_count)]
    small_sum = sum(part[:, 3 * own_width :].astype(f32) for part in front_parts)
    qkv_sum = in_rank_order([part[:, : 3 * own_width] for part in front_parts])
    qkv_sum = jnp.transpose(
        qkv_sum.reshape(seq_count, -1, 3, own_width), (1, 2, 0, 3)
    ).reshape(-1, 3 * model_width)
    out_sum = in_rank_order([from_peer(out_sum, step) for step in range(seq_count)])
    out_sum = jnp.transpose(out_sum, (1, 0, 2)).reshape(-1, model_width)
    return (
        block_out[None],
        grad_tokens[None],
        small_sum[:, 0],
        qkv_sum.astype(f32),
        small_sum[:, 1],
        small_sum[:, 2],
        out_sum.astype(f32),
        small_sum[:, 3],
        small_sum[:, 4:small_count],
        jnp.stack([rows[:up_rows] for rows in sums]).astype(f32),
        jnp.stack([rows[up_rows:] for rows in sums]).astype(f32),
    )


def solution(mesh):
    in_specs = (
        P("fsdp", "seq", None),
        P("fsdp", "seq", None),
        P("fsdp"),
        P("fsdp", "seq", None),
        P("fsdp"),
        P("fsdp", None),
        P("fsdp"),
        P("fsdp"),
        P("fsdp", None),
        P("fsdp"),
        P("fsdp", None),
        P("seq", "fsdp", None),
        P("seq", "fsdp", None),
    )
    out_specs = (
        P("fsdp", "seq", None),
        P("fsdp", "seq", None),
        P("fsdp"),
        P("fsdp", None),
        P("fsdp"),
        P("fsdp"),
        P("fsdp", None),
        P("fsdp"),
        P("fsdp", None),
        P("seq", "fsdp", None),
        P("seq", "fsdp", None),
    )
    return jax.shard_map(local, mesh=mesh, in_specs=in_specs, out_specs=out_specs, check_vma=False)
```

```python
from functools import partial

import jax
import jax.numpy as jnp
from jax import lax
from jax.sharding import PartitionSpec as P

HEADS = 16
HEAD = 128
TOP = 8
CAP = 136


EPSILON = 1e-05
ROPE_BASE = 10000.0
NEG_FILL = -1e30


def round_up(count, unit):
    return -(-count // unit) * unit


def rms_scale(values):
    return lax.rsqrt(jnp.mean(values * values, axis=-1, keepdims=True) + EPSILON)


def norm_back(grad_rows, unit_rows, scale_rows, gain_row):
    scaled = grad_rows * gain_row
    inner = jnp.mean(scaled * unit_rows, axis=-1, keepdims=True)
    return (scale_rows * (scaled - unit_rows * inner), jnp.sum(grad_rows * unit_rows, axis=0))


def rope_tables(positions):
    half_width = HEAD // 2
    frequency = ROPE_BASE ** (-(jnp.arange(half_width, dtype=jnp.float32) * 2.0 / HEAD))
    angles = positions[:, None] * frequency[None, :]
    return (
        jnp.concatenate([jnp.cos(angles), jnp.cos(angles)], -1),
        jnp.concatenate([jnp.sin(angles), jnp.sin(angles)], -1),
    )


def rotate(values, cosine_table, sine_table):
    half_width = values.shape[-1] // 2
    turned = jnp.concatenate([-values[..., half_width:], values[..., :half_width]], -1)
    return values * cosine_table[:, None, :] + turned * sine_table[:, None, :]


def rotate_back(grad_rows, cosine_table, sine_table):
    half_width = grad_rows.shape[-1] // 2
    sine_part = grad_rows * sine_table[:, None, :]
    return grad_rows * cosine_table[:, None, :] + jnp.concatenate(
        [sine_part[..., half_width:], -sine_part[..., :half_width]], -1
    )


def from_peer(values, step):
    if step == 0:
        return values
    count = lax.axis_size("seq")
    return lax.ppermute(values, "seq", [(rank, rank ^ step) for rank in range(count)])


def gather_blocks(values):
    return jnp.stack([from_peer(values, step) for step in range(lax.axis_size("seq"))])


def return_blocks(blocks):
    return [from_peer(blocks[step], step) for step in range(lax.axis_size("seq"))]


def in_rank_order(parts):
    seq_rank = lax.axis_index("seq")
    buffer = jnp.zeros((len(parts),) + parts[0].shape, parts[0].dtype)
    for step, part in enumerate(parts):
        start = (seq_rank ^ step,) + (0,) * part.ndim
        buffer = lax.dynamic_update_slice(buffer, part[None], start)
    return buffer


def attend_block(heads_in, places, length, row_count, block_start):
    queries, keys, values = heads_in
    query_block = lax.dynamic_slice_in_dim(queries, block_start, row_count, 0)
    query_place = lax.dynamic_slice_in_dim(places, block_start, row_count, 0)
    scores = jnp.einsum(
        "qhd,khd->hqk", query_block, keys, preferred_element_type=jnp.float32
    ) * HEAD ** (-0.5)
    allowed = (places[None, :] <= query_place[:, None]) & (places[None, :] < length)
    scores = jnp.where(allowed[None], scores, NEG_FILL)
    row_max = jnp.max(scores, axis=-1, keepdims=True)
    exp_scores = jnp.exp(scores - row_max)
    denom_sum = jnp.sum(exp_scores, axis=-1, keepdims=True)
    probabilities = (exp_scores / denom_sum).astype(jnp.bfloat16)
    attended = jnp.einsum("hqk,khd->qhd", probabilities, values, preferred_element_type=jnp.float32)
    return (attended.astype(jnp.bfloat16), jnp.transpose((row_max + jnp.log(denom_sum))[..., 0]))


def attend_back(heads_in, grad_heads, log_sums, places, length, row_count, carried, block_start):
    queries, keys, values = heads_in
    grad_keys, grad_values = carried
    score_scale = HEAD ** (-0.5)
    query_block = lax.dynamic_slice_in_dim(queries, block_start, row_count, 0)
    query_place = lax.dynamic_slice_in_dim(places, block_start, row_count, 0)
    grad_block = lax.dynamic_slice_in_dim(grad_heads, block_start, row_count, 0)
    sums_block = jnp.transpose(lax.dynamic_slice_in_dim(log_sums, block_start, row_count, 0))[
        :, :, None
    ]
    scores = (
        jnp.einsum("qhd,khd->hqk", query_block, keys, preferred_element_type=jnp.float32)
        * score_scale
    )
    allowed = (places[None, :] <= query_place[:, None]) & (places[None, :] < length)
    probabilities = jnp.where(allowed[None], jnp.exp(scores - sums_block), 0.0)
    low_probs = probabilities.astype(jnp.bfloat16)
    grad_probs = jnp.einsum("qhd,khd->hqk", grad_block, values, preferred_element_type=jnp.float32)
    grad_values = grad_values + jnp.einsum(
        "hqk,qhd->khd", low_probs, grad_block, preferred_element_type=jnp.float32
    )
    inner = jnp.sum(probabilities * grad_probs, axis=-1, keepdims=True)
    grad_scores = (probabilities * (grad_probs - inner)).astype(jnp.bfloat16)
    grad_query = (
        jnp.einsum("hqk,khd->qhd", grad_scores, keys, preferred_element_type=jnp.float32)
        * score_scale
    )
    grad_keys = (
        grad_keys
        + jnp.einsum("hqk,qhd->khd", grad_scores, query_block, preferred_element_type=jnp.float32)
        * score_scale
    )
    return ((grad_keys, grad_values), grad_query)


def mixed_dot(form, left, right):
    return jnp.einsum(form, left, right, preferred_element_type=jnp.float32)


def expert_forward(rows, grad_result_rows, slot_weight, gate_up, down):
    half_width = down.shape[0]
    gate_up_out = mixed_dot("rd,df->rf", rows, gate_up)
    gate_part = gate_up_out[:, :half_width]
    up_part = gate_up_out[:, half_width:]
    sigmoid_gate = jax.nn.sigmoid(gate_part)
    hidden = (gate_part * sigmoid_gate * up_part).astype(jnp.bfloat16)
    grad_result = (grad_result_rows.astype(jnp.float32) * slot_weight[:, None]).astype(jnp.bfloat16)
    grad_hidden = mixed_dot("rd,fd->rf", grad_result, down)
    grad_gate = grad_hidden * up_part * sigmoid_gate * (1.0 + gate_part * (1.0 - sigmoid_gate))
    grad_up = grad_hidden * gate_part * sigmoid_gate
    grad_mixed = jnp.concatenate([grad_gate, grad_up], -1).astype(jnp.bfloat16)
    grad_rows = mixed_dot("rd,fd->rf", grad_mixed, gate_up).astype(jnp.bfloat16)
    result = mixed_dot("rf,fd->rd", hidden, down).astype(jnp.bfloat16)
    grad_slot = jnp.sum(
        result.astype(jnp.float32) * grad_result_rows.astype(jnp.float32), axis=-1
    )
    weighted = (result.astype(jnp.float32) * slot_weight[:, None]).astype(jnp.bfloat16)
    return (weighted, grad_slot, grad_rows, (rows, grad_mixed, hidden, grad_result))


def expert_weights(kept):
    rows, grad_mixed, hidden, grad_result = kept
    grad_gate_up = mixed_dot("rd,rf->df", rows, grad_mixed).astype(jnp.bfloat16)
    grad_down = mixed_dot("rf,rd->fd", hidden, grad_result).astype(jnp.bfloat16)
    return (grad_gate_up, grad_down)


def after(values, *earlier):
    return lax.optimization_barrier((values, earlier))[0]


def split_rows(stacked, up_rows):
    count = lax.axis_size("fsdp")
    width = stacked.shape[-1]
    stacked = stacked.reshape(count, -1, width)
    return (stacked[:, :up_rows].reshape(-1, width), stacked[:, up_rows:].reshape(-1, width))


def chip_sums(gate_up, down):
    count = lax.axis_size("fsdp")
    core = lax.axis_index("fsdp") % 2
    width = gate_up.shape[-1]
    parts = [grad.reshape(count // 2, 2, -1, width) for grad in (gate_up, down)]

    def side(number):
        return jnp.concatenate(
            [lax.dynamic_index_in_dim(part, number, 1, False) for part in parts], axis=1
        )

    swapped = lax.ppermute(side(1 - core), "fsdp", [(index, index ^ 1) for index in range(count)])
    total = side(core).astype(jnp.float32) + swapped.astype(jnp.float32)
    return total.astype(gate_up.dtype).reshape(-1, width)


def scatter_chips(rows):
    count = lax.axis_size("fsdp")
    groups = [list(range(core, count, 2)) for core in range(2)]
    return lax.psum_scatter(
        rows, "fsdp", scatter_dimension=0, tiled=True, axis_index_groups=groups
    )


def local(
    tokens,
    cotangent,
    lengths,
    experts,
    attn_gain,
    qkv_weight,
    q_gain,
    k_gain,
    out_weight,
    moe_gain,
    router_weight,
    gate_up_weight,
    down_weight,
):
    bf16, f32 = jnp.bfloat16, jnp.float32
    seq_count = lax.axis_size("seq")
    seq_rank = lax.axis_index("seq")
    own_tokens = tokens[0]
    tok_count, model_width = own_tokens.shape
    local_count = gate_up_weight.shape[0]
    experts_count = local_count * seq_count
    own_width = model_width // seq_count
    own_heads = own_width // HEAD
    key_span = seq_count * tok_count
    length = lengths[0]
    block_ranks = seq_rank ^ jnp.arange(seq_count, dtype=jnp.int32)
    places = (
        block_ranks[:, None] * tok_count + jnp.arange(tok_count, dtype=jnp.int32)[None, :]
    ).reshape(-1)
    valid_all = (places < length).reshape(seq_count, tok_count)
    keep_mask = valid_all[0].astype(f32)[:, None]
    up_rows = gate_up_weight.shape[1]
    shards = [
        jnp.concatenate([gate_up_weight[index], down_weight[index]], axis=0)
        for index in range(local_count)
    ]

    own_qkv = lax.dynamic_index_in_dim(
        qkv_weight.reshape(-1, 3, seq_count, own_width), seq_rank, 2, False
    ).reshape(-1, 3 * own_width)
    own_small = jnp.concatenate(
        [jnp.stack([attn_gain, q_gain, k_gain, moe_gain], axis=1), router_weight], axis=1
    )
    small_count = 4 + experts_count
    small_width = round_up(small_count, 128)
    own_small = jnp.pad(own_small, ((0, 0), (0, small_width - small_count)))
    front = jnp.concatenate([own_qkv, own_small], axis=1)
    front_full = lax.all_gather(front, "fsdp", axis=0, tiled=True)
    token_blocks = gather_blocks(own_tokens)
    out_cut = lax.dynamic_slice_in_dim(out_weight, seq_rank * own_width, own_width, 1)
    out_cut = lax.all_gather(after(out_cut, front), "fsdp", axis=0, tiled=True)
    gather_expert = lambda index, *earlier: lax.all_gather(
        after(shards[index], *earlier), "fsdp", axis=0, tiled=True
    )
    weights = [gather_expert(0, front_full)]
    id_rows = experts[0].astype(bf16).reshape(-1, model_width)
    cot_parts = gather_blocks(
        after(jnp.concatenate([cotangent[0], id_rows], axis=0), token_blocks)
    )
    cot_blocks = cot_parts[:, :tok_count]
    id_blocks = cot_parts[:, tok_count:].reshape(seq_count, tok_count, -1).astype(jnp.int32)

    qkv_own = front_full[:, : 3 * own_width]
    small_full = front_full[:, 3 * own_width : 3 * own_width + small_count].T
    gain_one, gain_q, gain_k, gain_two = [small_full[i].astype(f32) for i in range(4)]
    router_rows = small_full[4:]
    gain_q = lax.dynamic_slice_in_dim(gain_q, seq_rank * own_width, own_width, 0)
    gain_k = lax.dynamic_slice_in_dim(gain_k, seq_rank * own_width, own_width, 0)
    inputs_all = token_blocks.reshape(key_span, model_width).astype(f32)
    scale_all = rms_scale(inputs_all)
    normed = (inputs_all * scale_all * gain_one).astype(bf16)
    projected = mixed_dot("td,de->te", normed, qkv_own)
    query_raw = projected[:, :own_width]
    key_raw = projected[:, own_width : 2 * own_width]
    value_raw = projected[:, 2 * own_width :]
    squares = jnp.stack([jnp.sum(query_raw * query_raw, -1), jnp.sum(key_raw * key_raw, -1)])

    def over_heads(parts):
        blocks = parts.reshape(2, seq_count, tok_count)
        total = blocks
        for step in range(1, seq_count):
            order = jnp.array([block ^ step for block in range(seq_count)])
            total = total + from_peer(blocks, step)[:, order]
        return total.reshape(2, key_span)

    scales = lax.rsqrt(over_heads(squares) / model_width + EPSILON)[:, :, None]
    unit_q = query_raw * scales[0]
    unit_k = key_raw * scales[1]
    cosine_table, sine_table = rope_tables(places.astype(f32))
    head_shape = (key_span, own_heads, HEAD)
    query_rot = rotate((unit_q * gain_q).reshape(head_shape), cosine_table, sine_table)
    key_rot = rotate((unit_k * gain_k).reshape(head_shape), cosine_table, sine_table)
    heads_in = (
        query_rot.astype(bf16),
        key_rot.astype(bf16),
        value_raw.reshape(head_shape).astype(bf16),
    )

    row_count = min(512, key_span)
    block_starts = jnp.arange(key_span // row_count, dtype=jnp.int32) * row_count
    attended_blocks, sums_blocks = lax.map(
        partial(attend_block, heads_in, places, length, row_count), block_starts
    )
    log_sums = sums_blocks.reshape(key_span, own_heads)
    weights.append(gather_expert(1, heads_in))
    out_cut = after(out_cut, heads_in)
    out_parts = [from_peer(out_cut, step) for step in range(seq_count)]

    out_full = in_rank_order(out_parts)
    attended_parts = return_blocks(attended_blocks.reshape(seq_count, tok_count, own_width))
    attended = jnp.transpose(in_rank_order(attended_parts), (1, 0, 2))
    inputs = own_tokens.astype(f32)
    branch = mixed_dot(
        "td,jdc->tjc", attended.reshape(tok_count, model_width), out_full
    ).reshape(tok_count, model_width)
    middle = inputs + branch * keep_mask
    scale_two = rms_scale(middle)
    unit_two = middle * scale_two
    normed_two = (unit_two * gain_two).astype(bf16)

    row_blocks = gather_blocks(normed_two)
    weights.append(gather_expert(2, normed_two))
    weights += [gather_expert(index, row_blocks) for index in range(3, local_count)]
    logits = mixed_dot("btd,ed->bte", row_blocks, router_rows)
    expert_range = jnp.arange(experts_count, dtype=jnp.int32)
    named = jnp.any(id_blocks[..., None] == expert_range, axis=2)
    chosen = jnp.where(named, logits, NEG_FILL)
    exp_chosen = jnp.where(named, jnp.exp(chosen - jnp.max(chosen, -1, keepdims=True)), 0.0)
    gates = exp_chosen / jnp.sum(exp_chosen, axis=-1, keepdims=True)
    routed = (named & valid_all[..., None]).astype(jnp.int32)
    before = jnp.cumsum(routed, axis=1) - routed
    local_routed = lax.dynamic_slice_in_dim(routed, seq_rank * local_count, local_count, 2)
    local_before = lax.dynamic_slice_in_dim(before, seq_rank * local_count, local_count, 2)
    local_gates = lax.dynamic_slice_in_dim(gates, seq_rank * local_count, local_count, 2)
    slot_count = round_up(CAP, 16)
    slot_place = jnp.where(local_routed == 1, local_before, -1)
    slot_place = jnp.transpose(slot_place, (2, 0, 1))
    local_gates = jnp.transpose(local_gates, (2, 0, 1))
    slot_hit = slot_place[:, :, None, :] == jnp.arange(slot_count, dtype=jnp.int32)[:, None]
    slot_pick = slot_hit.astype(bf16)
    slot_gates = jnp.sum(jnp.where(slot_hit, local_gates[:, :, None, :], 0.0), axis=-1)

    def picked(index):
        return tuple(
            mixed_dot("bct,btd->bcd", slot_pick[index], blocks)
            .astype(bf16)
            .reshape(seq_count * slot_count, model_width)
            for blocks in (row_blocks, cot_blocks)
        )

    def computed(index, pair):
        weighted, grad_slot, grad_rows, kept = expert_forward(
            *pair, slot_gates[index].reshape(-1), *split_rows(weights[index], up_rows)
        )
        weighted_rows.append(weighted.reshape(seq_count, slot_count, model_width))
        grad_row_sets.append(grad_rows.reshape(seq_count, slot_count, model_width))
        grad_slots.append(
            jnp.sum(
                jnp.where(
                    slot_hit[index], grad_slot.reshape(seq_count, slot_count)[:, :, None], 0.0
                ),
                1,
            )
        )
        return kept

    weighted_rows, grad_row_sets, grad_slots, sums = [], [], [], []
    scatter = lambda grads: lax.psum_scatter(grads, "fsdp", scatter_dimension=0, tiled=True)
    pair = picked(0)
    for index in range(local_count):
        kept = computed(index, pair)
        if index + 1 < local_count:
            grads = chip_sums(*expert_weights(kept))
            pair = after(picked(index + 1), grads)
            if index + 2 < local_count:
                sums.append(scatter_chips(grads))
    pick_all = jnp.concatenate([slot_pick[index] for index in range(local_count)], axis=1)
    grad_partial = mixed_dot("bct,bcd->btd", pick_all, jnp.concatenate(grad_row_sets, axis=1))

    grad_gates = return_blocks(jnp.stack(grad_slots, axis=1))
    grad_back = return_blocks(grad_partial.astype(bf16))
    moe_partial = mixed_dot("bct,bcd->btd", pick_all, jnp.concatenate(weighted_rows, axis=1))
    last_grads = expert_weights(kept)
    grad_back = after(grad_back, last_grads, moe_partial.astype(bf16))

    own_gates = gates[0]
    grad_gates = jnp.transpose(in_rank_order(grad_gates), (2, 0, 1)).reshape(
        tok_count, experts_count
    )
    grad_logits = own_gates * (
        grad_gates - jnp.sum(own_gates * grad_gates, axis=-1, keepdims=True)
    )
    grad_out = cotangent[0].astype(f32) * keep_mask
    grad_normed_two = jnp.einsum(
        "te,ed->td", grad_logits, router_rows.astype(f32), precision=lax.Precision.HIGHEST
    ) + sum(part.astype(f32) for part in grad_back)
    grad_router = jnp.einsum(
        "te,td->ed", grad_logits, normed_two.astype(f32), precision=lax.Precision.HIGHEST
    )
    grad_middle_norm, grad_two = norm_back(grad_normed_two, unit_two, scale_two, gain_two)
    grad_middle = grad_out + grad_middle_norm
    grad_branch = (grad_middle * keep_mask).astype(bf16)
    grad_attended = mixed_dot(
        "tjc,jdc->td", grad_branch.reshape(tok_count, seq_count, own_width), out_full
    ).astype(bf16)
    cut_heads = grad_attended.reshape(tok_count, seq_count, own_width)
    grad_heads = jnp.stack(
        [
            from_peer(lax.dynamic_index_in_dim(cut_heads, seq_rank ^ step, 1, False), step)
            for step in range(seq_count)
        ]
    ).reshape(head_shape)

    sums.append(scatter_chips(after(grads, grad_heads, *sums[:1])))
    moe_parts = return_blocks(after(moe_partial.astype(bf16), grad_heads))
    zero_heads = jnp.zeros(head_shape, f32)
    (grad_keys, grad_values), grad_queries = lax.scan(
        partial(attend_back, heads_in, grad_heads, log_sums, places, length, row_count),
        (zero_heads, zero_heads),
        block_starts,
    )

    grad_queries = after(grad_queries, moe_parts)
    low = lambda rows: rows.reshape(head_shape).astype(bf16).astype(f32)
    grad_qn = rotate_back(low(grad_queries), cosine_table, sine_table).reshape(key_span, own_width)
    grad_kn = rotate_back(low(grad_keys), cosine_table, sine_table).reshape(key_span, own_width)
    scaled_q = grad_qn * gain_q
    scaled_k = grad_kn * gain_k
    inners = over_heads(
        jnp.stack([jnp.sum(scaled_q * unit_q, -1), jnp.sum(scaled_k * unit_k, -1)])
    )
    grad_branch = after(grad_branch, inners)
    grad_cut = mixed_dot("td,tc->dc", attended.reshape(tok_count, model_width), grad_branch)
    grad_cut = grad_cut.astype(bf16).reshape(model_width, seq_count, own_width)
    grad_cut = [
        lax.dynamic_index_in_dim(grad_cut, seq_rank ^ step, 1, False) for step in range(seq_count)
    ]
    near_cuts = [from_peer(grad_cut[step], step) for step in range(min(3, seq_count))]
    far_cuts = [
        from_peer(after(grad_cut[step], near_cuts), step) for step in range(3, seq_count)
    ]
    inners = (inners / model_width)[:, :, None]
    grad_projected = jnp.concatenate(
        [
            scales[0] * (scaled_q - unit_q * inners[0]),
            scales[1] * (scaled_k - unit_k * inners[1]),
            grad_values.reshape(key_span, own_width),
        ],
        axis=1,
    ).astype(bf16)
    grad_normed = mixed_dot("te,de->td", grad_projected, qkv_own)
    grad_one = jnp.sum(grad_normed * (inputs_all * scale_all), axis=0)
    grad_qkv = mixed_dot("td,te->de", normed, grad_projected).astype(bf16)
    placed = lambda row: lax.dynamic_update_slice(
        jnp.zeros((model_width,), f32), row, (seq_rank * own_width,)
    )
    grad_small = jnp.concatenate(
        [
            jnp.stack(
                [
                    grad_one,
                    placed(jnp.sum(grad_qn * unit_q, axis=0)),
                    placed(jnp.sum(grad_kn * unit_k, axis=0)),
                    grad_two,
                ]
            ),
            grad_router,
            jnp.zeros((small_width - small_count, model_width), f32),
        ],
        axis=0,
    )
    grad_front = jnp.concatenate([grad_qkv, grad_small.T.astype(bf16)], axis=1)
    grad_front = after(grad_front, near_cuts)

    front_sum = scatter(after(grad_front, *sums[:-1]))
    grad_cut = sum(part.astype(f32) for part in near_cuts + far_cuts).astype(bf16)
    out_sum = scatter(after(grad_cut, *sums, grad_front))
    last_grads = chip_sums(*after(last_grads, grad_front))
    grad_normed = return_blocks(grad_normed.astype(bf16).reshape(seq_count, tok_count, model_width))
    front_parts = [from_peer(front_sum, step) for step in range(seq_count)]
    block_out = (middle + sum(part.astype(f32) for part in moe_parts)).astype(bf16)
    grad_normed = sum(part.astype(f32) for part in grad_normed)
    scale_one = rms_scale(inputs)
    scaled = grad_normed * gain_one
    unit_one = inputs * scale_one
    inner = jnp.mean(scaled * unit_one, axis=-1, keepdims=True)
    grad_tokens = (grad_middle + scale_one * (scaled - unit_one * inner)).astype(bf16)
    small_sum = sum(part[:, 3 * own_width :].astype(f32) for part in front_parts)
    qkv_sum = in_rank_order([part[:, : 3 * own_width] for part in front_parts])
    qkv_sum = jnp.transpose(
        qkv_sum.reshape(seq_count, -1, 3, own_width), (1, 2, 0, 3)
    ).reshape(-1, 3 * model_width)
    out_sum = in_rank_order([from_peer(out_sum, step) for step in range(seq_count)])
    out_sum = jnp.transpose(out_sum, (1, 0, 2)).reshape(-1, model_width)
    last_sum = scatter_chips(after(last_grads, front_sum))
    qkv_sum, out_sum = qkv_sum.astype(f32), out_sum.astype(f32)
    up_sums = jnp.zeros((local_count, up_rows, model_width), f32)
    down_sums = jnp.zeros((local_count,) + down_weight.shape[1:], f32)
    for index in range(local_count):
        if index + 1 == local_count:
            last_sum, up_sums, down_sums, block_out, grad_tokens, qkv_sum, out_sum = (
                lax.optimization_barrier(
                    (last_sum, up_sums, down_sums, block_out, grad_tokens, qkv_sum, out_sum)
                )
            )
        rows = (sums[index] if index + 1 < local_count else last_sum).astype(f32)
        up_sums = lax.dynamic_update_slice(up_sums, rows[None, :up_rows], (index, 0, 0))
        down_sums = lax.dynamic_update_slice(down_sums, rows[None, up_rows:], (index, 0, 0))
    return (
        block_out[None],
        grad_tokens[None],
        small_sum[:, 0],
        qkv_sum,
        small_sum[:, 1],
        small_sum[:, 2],
        out_sum,
        small_sum[:, 3],
        small_sum[:, 4:small_count],
        up_sums,
        down_sums,
    )


def solution(mesh):
    in_specs = (
        P("fsdp", "seq", None),
        P("fsdp", "seq", None),
        P("fsdp"),
        P("fsdp", "seq", None),
        P("fsdp"),
        P("fsdp", None),
        P("fsdp"),
        P("fsdp"),
        P("fsdp", None),
        P("fsdp"),
        P("fsdp", None),
        P("seq", "fsdp", None),
        P("seq", "fsdp", None),
    )
    out_specs = (
        P("fsdp", "seq", None),
        P("fsdp", "seq", None),
        P("fsdp"),
        P("fsdp", None),
        P("fsdp"),
        P("fsdp"),
        P("fsdp", None),
        P("fsdp"),
        P("fsdp", None),
        P("seq", "fsdp", None),
        P("seq", "fsdp", None),
    )
    return jax.shard_map(local, mesh=mesh, in_specs=in_specs, out_specs=out_specs, check_vma=False)
```

```python
from functools import partial

import jax
import jax.numpy as jnp
from jax import lax
from jax.sharding import PartitionSpec as P

HEADS = 16
HEAD = 128
TOP = 8
CAP = 136


EPSILON = 1e-05
ROPE_BASE = 10000.0
NEG_FILL = -1e30


def round_up(count, unit):
    return -(-count // unit) * unit


def rms_scale(values):
    return lax.rsqrt(jnp.mean(values * values, axis=-1, keepdims=True) + EPSILON)


def norm_back(grad_rows, unit_rows, scale_rows, gain_row):
    scaled = grad_rows * gain_row
    inner = jnp.mean(scaled * unit_rows, axis=-1, keepdims=True)
    return (scale_rows * (scaled - unit_rows * inner), jnp.sum(grad_rows * unit_rows, axis=0))


def rope_tables(positions):
    half_width = HEAD // 2
    frequency = ROPE_BASE ** (-(jnp.arange(half_width, dtype=jnp.float32) * 2.0 / HEAD))
    angles = positions[:, None] * frequency[None, :]
    return (
        jnp.concatenate([jnp.cos(angles), jnp.cos(angles)], -1),
        jnp.concatenate([jnp.sin(angles), jnp.sin(angles)], -1),
    )


def rotate(values, cosine_table, sine_table):
    half_width = values.shape[-1] // 2
    turned = jnp.concatenate([-values[..., half_width:], values[..., :half_width]], -1)
    return values * cosine_table[:, None, :] + turned * sine_table[:, None, :]


def rotate_back(grad_rows, cosine_table, sine_table):
    half_width = grad_rows.shape[-1] // 2
    sine_part = grad_rows * sine_table[:, None, :]
    return grad_rows * cosine_table[:, None, :] + jnp.concatenate(
        [sine_part[..., half_width:], -sine_part[..., :half_width]], -1
    )


def from_peer(values, step):
    if step == 0:
        return values
    count = lax.axis_size("seq")
    return lax.ppermute(values, "seq", [(rank, rank ^ step) for rank in range(count)])


def gather_blocks(values):
    return jnp.stack([from_peer(values, step) for step in range(lax.axis_size("seq"))])


def return_blocks(blocks):
    return [from_peer(blocks[step], step) for step in range(lax.axis_size("seq"))]


def in_rank_order(parts):
    seq_rank = lax.axis_index("seq")
    buffer = jnp.zeros((len(parts),) + parts[0].shape, parts[0].dtype)
    for step, part in enumerate(parts):
        start = (seq_rank ^ step,) + (0,) * part.ndim
        buffer = lax.dynamic_update_slice(buffer, part[None], start)
    return buffer


def attend_block(heads_in, places, length, row_count, block_start):
    queries, keys, values = heads_in
    query_block = lax.dynamic_slice_in_dim(queries, block_start, row_count, 0)
    query_place = lax.dynamic_slice_in_dim(places, block_start, row_count, 0)
    scores = jnp.einsum(
        "qhd,khd->hqk", query_block, keys, preferred_element_type=jnp.float32
    ) * HEAD ** (-0.5)
    allowed = (places[None, :] <= query_place[:, None]) & (places[None, :] < length)
    scores = jnp.where(allowed[None], scores, NEG_FILL)
    row_max = jnp.max(scores, axis=-1, keepdims=True)
    exp_scores = jnp.exp(scores - row_max)
    denom_sum = jnp.sum(exp_scores, axis=-1, keepdims=True)
    probabilities = (exp_scores / denom_sum).astype(jnp.bfloat16)
    attended = jnp.einsum("hqk,khd->qhd", probabilities, values, preferred_element_type=jnp.float32)
    return (attended.astype(jnp.bfloat16), jnp.transpose((row_max + jnp.log(denom_sum))[..., 0]))


def attend_back(heads_in, grad_heads, log_sums, places, length, row_count, carried, block_start):
    queries, keys, values = heads_in
    grad_keys, grad_values = carried
    score_scale = HEAD ** (-0.5)
    query_block = lax.dynamic_slice_in_dim(queries, block_start, row_count, 0)
    query_place = lax.dynamic_slice_in_dim(places, block_start, row_count, 0)
    grad_block = lax.dynamic_slice_in_dim(grad_heads, block_start, row_count, 0)
    sums_block = jnp.transpose(lax.dynamic_slice_in_dim(log_sums, block_start, row_count, 0))[
        :, :, None
    ]
    scores = (
        jnp.einsum("qhd,khd->hqk", query_block, keys, preferred_element_type=jnp.float32)
        * score_scale
    )
    allowed = (places[None, :] <= query_place[:, None]) & (places[None, :] < length)
    probabilities = jnp.where(allowed[None], jnp.exp(scores - sums_block), 0.0)
    low_probs = probabilities.astype(jnp.bfloat16)
    grad_probs = jnp.einsum("qhd,khd->hqk", grad_block, values, preferred_element_type=jnp.float32)
    grad_values = grad_values + jnp.einsum(
        "hqk,qhd->khd", low_probs, grad_block, preferred_element_type=jnp.float32
    )
    inner = jnp.sum(probabilities * grad_probs, axis=-1, keepdims=True)
    grad_scores = (probabilities * (grad_probs - inner)).astype(jnp.bfloat16)
    grad_query = (
        jnp.einsum("hqk,khd->qhd", grad_scores, keys, preferred_element_type=jnp.float32)
        * score_scale
    )
    grad_keys = (
        grad_keys
        + jnp.einsum("hqk,qhd->khd", grad_scores, query_block, preferred_element_type=jnp.float32)
        * score_scale
    )
    return ((grad_keys, grad_values), grad_query)


def mixed_dot(form, left, right):
    return jnp.einsum(form, left, right, preferred_element_type=jnp.float32)


def expert_forward(rows, grad_result_rows, slot_weight, gate_up, down):
    half_width = down.shape[0]
    gate_up_out = mixed_dot("rd,df->rf", rows, gate_up)
    gate_part = gate_up_out[:, :half_width]
    up_part = gate_up_out[:, half_width:]
    sigmoid_gate = jax.nn.sigmoid(gate_part)
    hidden = (gate_part * sigmoid_gate * up_part).astype(jnp.bfloat16)
    grad_result = (grad_result_rows.astype(jnp.float32) * slot_weight[:, None]).astype(jnp.bfloat16)
    grad_hidden = mixed_dot("rd,fd->rf", grad_result, down)
    grad_gate = grad_hidden * up_part * sigmoid_gate * (1.0 + gate_part * (1.0 - sigmoid_gate))
    grad_up = grad_hidden * gate_part * sigmoid_gate
    grad_mixed = jnp.concatenate([grad_gate, grad_up], -1).astype(jnp.bfloat16)
    grad_rows = mixed_dot("rd,fd->rf", grad_mixed, gate_up).astype(jnp.bfloat16)
    result = mixed_dot("rf,fd->rd", hidden, down).astype(jnp.bfloat16)
    grad_slot = jnp.sum(
        result.astype(jnp.float32) * grad_result_rows.astype(jnp.float32), axis=-1
    )
    weighted = (result.astype(jnp.float32) * slot_weight[:, None]).astype(jnp.bfloat16)
    return (weighted, grad_slot, grad_rows, (rows, grad_mixed, hidden, grad_result))


def expert_weights(kept):
    rows, grad_mixed, hidden, grad_result = kept
    grad_gate_up = mixed_dot("rd,rf->df", rows, grad_mixed).astype(jnp.bfloat16)
    grad_down = mixed_dot("rf,rd->fd", hidden, grad_result).astype(jnp.bfloat16)
    return (grad_gate_up, grad_down)


def after(values, *earlier):
    return lax.optimization_barrier((values, earlier))[0]


def split_rows(stacked, up_rows):
    count = lax.axis_size("fsdp")
    width = stacked.shape[-1]
    stacked = stacked.reshape(count, -1, width)
    return (stacked[:, :up_rows].reshape(-1, width), stacked[:, up_rows:].reshape(-1, width))


def chip_sums(gate_up, down):
    count = lax.axis_size("fsdp")
    core = lax.axis_index("fsdp") % 2
    width = gate_up.shape[-1]
    parts = [grad.reshape(count // 2, 2, -1, width) for grad in (gate_up, down)]

    def side(number):
        return jnp.concatenate(
            [lax.dynamic_index_in_dim(part, number, 1, False) for part in parts], axis=1
        )

    swapped = lax.ppermute(side(1 - core), "fsdp", [(index, index ^ 1) for index in range(count)])
    total = side(core).astype(jnp.float32) + swapped.astype(jnp.float32)
    return total.astype(gate_up.dtype).reshape(-1, width)


def scatter_chips(rows):
    count = lax.axis_size("fsdp")
    groups = [list(range(core, count, 2)) for core in range(2)]
    return lax.psum_scatter(
        rows, "fsdp", scatter_dimension=0, tiled=True, axis_index_groups=groups
    )


def local(
    tokens,
    cotangent,
    lengths,
    experts,
    attn_gain,
    qkv_weight,
    q_gain,
    k_gain,
    out_weight,
    moe_gain,
    router_weight,
    gate_up_weight,
    down_weight,
):
    bf16, f32 = jnp.bfloat16, jnp.float32
    seq_count = lax.axis_size("seq")
    seq_rank = lax.axis_index("seq")
    own_tokens = tokens[0]
    tok_count, model_width = own_tokens.shape
    local_count = gate_up_weight.shape[0]
    experts_count = local_count * seq_count
    own_width = model_width // seq_count
    own_heads = own_width // HEAD
    key_span = seq_count * tok_count
    length = lengths[0]
    block_ranks = seq_rank ^ jnp.arange(seq_count, dtype=jnp.int32)
    places = (
        block_ranks[:, None] * tok_count + jnp.arange(tok_count, dtype=jnp.int32)[None, :]
    ).reshape(-1)
    valid_all = (places < length).reshape(seq_count, tok_count)
    keep_mask = valid_all[0].astype(f32)[:, None]
    up_rows = gate_up_weight.shape[1]
    shards = [
        jnp.concatenate([gate_up_weight[index], down_weight[index]], axis=0)
        for index in range(local_count)
    ]

    own_qkv = [
        lax.dynamic_slice_in_dim(
            qkv_weight, kind * model_width + seq_rank * own_width, own_width, 1
        )
        for kind in range(3)
    ]
    own_small = jnp.concatenate(
        [jnp.stack([attn_gain, q_gain, k_gain, moe_gain], axis=1), router_weight], axis=1
    )
    small_count = 4 + experts_count
    small_width = round_up(small_count, 32)
    own_small = jnp.pad(own_small, ((0, 0), (0, small_width - small_count)))
    front = jnp.concatenate(own_qkv + [own_small], axis=1)
    front_full = lax.all_gather(front, "fsdp", axis=0, tiled=True)
    token_blocks = gather_blocks(own_tokens)
    out_cut = lax.dynamic_slice_in_dim(out_weight, seq_rank * own_width, own_width, 1)
    out_cut = lax.all_gather(after(out_cut, front), "fsdp", axis=0, tiled=True)
    gather_expert = lambda index, *earlier: lax.all_gather(
        after(shards[index], *earlier), "fsdp", axis=0, tiled=True
    )
    weights = [gather_expert(0, front_full)]
    id_rows = experts[0].astype(bf16).reshape(-1, model_width)
    cot_parts = gather_blocks(
        after(jnp.concatenate([cotangent[0], id_rows], axis=0), token_blocks)
    )
    cot_blocks = cot_parts[:, :tok_count]
    id_blocks = cot_parts[:, tok_count:].reshape(seq_count, tok_count, -1).astype(jnp.int32)

    qkv_own = front_full[:, : 3 * own_width]
    small_full = front_full[:, 3 * own_width : 3 * own_width + small_count].T
    gain_one, gain_q, gain_k, gain_two = [small_full[i].astype(f32) for i in range(4)]
    router_rows = small_full[4:]
    gain_q = lax.dynamic_slice_in_dim(gain_q, seq_rank * own_width, own_width, 0)
    gain_k = lax.dynamic_slice_in_dim(gain_k, seq_rank * own_width, own_width, 0)
    inputs_all = token_blocks.reshape(key_span, model_width).astype(f32)
    scale_all = rms_scale(inputs_all)
    normed = (inputs_all * scale_all * gain_one).astype(bf16)
    projected = mixed_dot("td,de->te", normed, qkv_own)
    query_raw = projected[:, :own_width]
    key_raw = projected[:, own_width : 2 * own_width]
    value_raw = projected[:, 2 * own_width :]
    squares = jnp.stack([jnp.sum(query_raw * query_raw, -1), jnp.sum(key_raw * key_raw, -1)])

    def over_heads(parts):
        blocks = parts.reshape(2, seq_count, tok_count)
        total = blocks
        for step in range(1, seq_count):
            order = jnp.array([block ^ step for block in range(seq_count)])
            total = total + from_peer(blocks, step)[:, order]
        return total.reshape(2, key_span)

    scales = lax.rsqrt(over_heads(squares) / model_width + EPSILON)[:, :, None]
    unit_q = query_raw * scales[0]
    unit_k = key_raw * scales[1]
    cosine_table, sine_table = rope_tables(places.astype(f32))
    head_shape = (key_span, own_heads, HEAD)
    query_rot = rotate((unit_q * gain_q).reshape(head_shape), cosine_table, sine_table)
    key_rot = rotate((unit_k * gain_k).reshape(head_shape), cosine_table, sine_table)
    heads_in = (
        query_rot.astype(bf16),
        key_rot.astype(bf16),
        value_raw.reshape(head_shape).astype(bf16),
    )

    row_count = min(512, key_span)
    block_starts = jnp.arange(key_span // row_count, dtype=jnp.int32) * row_count
    attended_blocks, sums_blocks = lax.map(
        partial(attend_block, heads_in, places, length, row_count), block_starts
    )
    log_sums = sums_blocks.reshape(key_span, own_heads)
    weights.append(gather_expert(1, heads_in))
    out_cut = after(out_cut, heads_in)
    out_parts = [from_peer(out_cut, step) for step in range(seq_count)]

    out_full = in_rank_order(out_parts)
    attended_parts = return_blocks(attended_blocks.reshape(seq_count, tok_count, own_width))
    attended = jnp.transpose(in_rank_order(attended_parts), (1, 0, 2))
    inputs = own_tokens.astype(f32)
    branch = mixed_dot(
        "td,jdc->tjc", attended.reshape(tok_count, model_width), out_full
    ).reshape(tok_count, model_width)
    middle = inputs + branch * keep_mask
    scale_two = rms_scale(middle)
    unit_two = middle * scale_two
    normed_two = (unit_two * gain_two).astype(bf16)

    row_blocks = gather_blocks(normed_two)
    weights.append(gather_expert(2, normed_two))
    weights += [gather_expert(index, row_blocks) for index in range(3, local_count)]
    logits = mixed_dot("btd,ed->bte", row_blocks, router_rows)
    expert_range = jnp.arange(experts_count, dtype=jnp.int32)
    named = jnp.any(id_blocks[..., None] == expert_range, axis=2)
    chosen = jnp.where(named, logits, NEG_FILL)
    exp_chosen = jnp.where(named, jnp.exp(chosen - jnp.max(chosen, -1, keepdims=True)), 0.0)
    gates = exp_chosen / jnp.sum(exp_chosen, axis=-1, keepdims=True)
    routed = (named & valid_all[..., None]).astype(jnp.int32)
    before = jnp.cumsum(routed, axis=1) - routed
    local_routed = lax.dynamic_slice_in_dim(routed, seq_rank * local_count, local_count, 2)
    local_before = lax.dynamic_slice_in_dim(before, seq_rank * local_count, local_count, 2)
    local_gates = lax.dynamic_slice_in_dim(gates, seq_rank * local_count, local_count, 2)
    slot_count = round_up(CAP, 16)
    slot_place = jnp.where(local_routed == 1, local_before, -1)
    slot_place = jnp.transpose(slot_place, (2, 0, 1))
    local_gates = jnp.transpose(local_gates, (2, 0, 1))
    slot_hit = slot_place[:, :, None, :] == jnp.arange(slot_count, dtype=jnp.int32)[:, None]
    slot_pick = slot_hit.astype(bf16)
    slot_gates = jnp.sum(jnp.where(slot_hit, local_gates[:, :, None, :], 0.0), axis=-1)

    def picked(index):
        return tuple(
            mixed_dot("bct,btd->bcd", slot_pick[index], blocks)
            .astype(bf16)
            .reshape(seq_count * slot_count, model_width)
            for blocks in (row_blocks, cot_blocks)
        )

    def computed(index, pair):
        weighted, grad_slot, grad_rows, kept = expert_forward(
            *pair, slot_gates[index].reshape(-1), *split_rows(weights[index], up_rows)
        )
        weighted_rows.append(weighted.reshape(seq_count, slot_count, model_width))
        grad_row_sets.append(grad_rows.reshape(seq_count, slot_count, model_width))
        grad_slots.append(
            jnp.sum(
                jnp.where(
                    slot_hit[index], grad_slot.reshape(seq_count, slot_count)[:, :, None], 0.0
                ),
                1,
            )
        )
        return kept

    weighted_rows, grad_row_sets, grad_slots, sums = [], [], [], []
    scatter = lambda grads: lax.psum_scatter(grads, "fsdp", scatter_dimension=0, tiled=True)
    pair = picked(0)
    for index in range(local_count):
        kept = computed(index, pair)
        if index + 1 < local_count:
            grads = chip_sums(*expert_weights(kept))
            pair = after(picked(index + 1), grads)
            if index + 2 < local_count:
                sums.append(scatter_chips(grads))
    pick_all = jnp.concatenate([slot_pick[index] for index in range(local_count)], axis=1)
    grad_partial = mixed_dot("bct,bcd->btd", pick_all, jnp.concatenate(grad_row_sets, axis=1))

    grad_gates = return_blocks(jnp.stack(grad_slots, axis=1))
    grad_back = return_blocks(grad_partial.astype(bf16))
    moe_partial = mixed_dot("bct,bcd->btd", pick_all, jnp.concatenate(weighted_rows, axis=1))
    last_grads = expert_weights(kept)
    grad_back = after(grad_back, last_grads, moe_partial.astype(bf16))

    own_gates = gates[0]
    grad_gates = jnp.transpose(in_rank_order(grad_gates), (2, 0, 1)).reshape(
        tok_count, experts_count
    )
    grad_logits = own_gates * (
        grad_gates - jnp.sum(own_gates * grad_gates, axis=-1, keepdims=True)
    )
    grad_out = cotangent[0].astype(f32) * keep_mask
    grad_normed_two = jnp.einsum(
        "te,ed->td", grad_logits, router_rows.astype(f32), precision=lax.Precision.HIGHEST
    ) + sum(part.astype(f32) for part in grad_back)
    grad_router = jnp.einsum(
        "te,td->ed", grad_logits, normed_two.astype(f32), precision=lax.Precision.HIGHEST
    )
    grad_middle_norm, grad_two = norm_back(grad_normed_two, unit_two, scale_two, gain_two)
    grad_middle = grad_out + grad_middle_norm
    grad_branch = (grad_middle * keep_mask).astype(bf16)
    grad_attended = mixed_dot(
        "tjc,jdc->td", grad_branch.reshape(tok_count, seq_count, own_width), out_full
    ).astype(bf16)
    cut_heads = grad_attended.reshape(tok_count, seq_count, own_width)
    grad_heads = jnp.stack(
        [
            from_peer(lax.dynamic_index_in_dim(cut_heads, seq_rank ^ step, 1, False), step)
            for step in range(seq_count)
        ]
    ).reshape(head_shape)

    sums.append(scatter_chips(after(grads, grad_heads, *sums[:1])))
    moe_parts = return_blocks(after(moe_partial.astype(bf16), grad_heads))
    zero_heads = jnp.zeros(head_shape, f32)
    (grad_keys, grad_values), grad_queries = lax.scan(
        partial(attend_back, heads_in, grad_heads, log_sums, places, length, row_count),
        (zero_heads, zero_heads),
        block_starts,
    )

    grad_queries = after(grad_queries, moe_parts)
    low = lambda rows: rows.reshape(head_shape).astype(bf16).astype(f32)
    grad_qn = rotate_back(low(grad_queries), cosine_table, sine_table).reshape(key_span, own_width)
    grad_kn = rotate_back(low(grad_keys), cosine_table, sine_table).reshape(key_span, own_width)
    scaled_q = grad_qn * gain_q
    scaled_k = grad_kn * gain_k
    inners = over_heads(
        jnp.stack([jnp.sum(scaled_q * unit_q, -1), jnp.sum(scaled_k * unit_k, -1)])
    )
    grad_branch = after(grad_branch, inners)
    grad_cut = mixed_dot("td,tc->dc", attended.reshape(tok_count, model_width), grad_branch)
    grad_cut = grad_cut.astype(bf16).reshape(model_width, seq_count, own_width)
    grad_cut = [
        lax.dynamic_index_in_dim(grad_cut, seq_rank ^ step, 1, False) for step in range(seq_count)
    ]
    near_cuts = [from_peer(grad_cut[step], step) for step in range(min(3, seq_count))]
    far_cuts = [
        from_peer(after(grad_cut[step], near_cuts), step) for step in range(3, seq_count)
    ]
    inners = (inners / model_width)[:, :, None]
    grad_projected = jnp.concatenate(
        [
            scales[0] * (scaled_q - unit_q * inners[0]),
            scales[1] * (scaled_k - unit_k * inners[1]),
            grad_values.reshape(key_span, own_width),
        ],
        axis=1,
    ).astype(bf16)
    grad_normed = mixed_dot("te,de->td", grad_projected, qkv_own)
    grad_one = jnp.sum(grad_normed * (inputs_all * scale_all), axis=0)
    grad_qkv = mixed_dot("td,te->de", normed, grad_projected).astype(bf16)
    placed = lambda row: lax.dynamic_update_slice(
        jnp.zeros((model_width,), f32), row, (seq_rank * own_width,)
    )
    grad_small = jnp.concatenate(
        [
            jnp.stack(
                [
                    grad_one,
                    placed(jnp.sum(grad_qn * unit_q, axis=0)),
                    placed(jnp.sum(grad_kn * unit_k, axis=0)),
                    grad_two,
                ]
            ),
            grad_router,
            jnp.zeros((small_width - small_count, model_width), f32),
        ],
        axis=0,
    )
    grad_front = jnp.concatenate([grad_qkv, grad_small.T.astype(bf16)], axis=1)
    grad_front = after(grad_front, near_cuts)

    front_sum = scatter(after(grad_front, *sums[:-1]))
    grad_cut = sum(part.astype(f32) for part in near_cuts + far_cuts).astype(bf16)
    out_sum = scatter(after(grad_cut, *sums, grad_front))
    last_grads = chip_sums(*after(last_grads, grad_front))
    grad_normed = return_blocks(grad_normed.astype(bf16).reshape(seq_count, tok_count, model_width))
    front_parts = [from_peer(front_sum, step) for step in range(seq_count)]
    block_out = (middle + sum(part.astype(f32) for part in moe_parts)).astype(bf16)
    grad_normed = sum(part.astype(f32) for part in grad_normed)
    scale_one = rms_scale(inputs)
    scaled = grad_normed * gain_one
    unit_one = inputs * scale_one
    inner = jnp.mean(scaled * unit_one, axis=-1, keepdims=True)
    grad_tokens = (grad_middle + scale_one * (scaled - unit_one * inner)).astype(bf16)
    small_sum = sum(part[:, 3 * own_width :].astype(f32) for part in front_parts)
    qkv_sum = in_rank_order([part[:, : 3 * own_width] for part in front_parts])
    qkv_sum = jnp.transpose(
        qkv_sum.reshape(seq_count, -1, 3, own_width), (1, 2, 0, 3)
    ).reshape(-1, 3 * model_width)
    out_sum = in_rank_order([from_peer(out_sum, step) for step in range(seq_count)])
    out_sum = jnp.transpose(out_sum, (1, 0, 2)).reshape(-1, model_width)
    last_sum = scatter_chips(after(last_grads, front_sum))
    qkv_sum, out_sum = qkv_sum.astype(f32), out_sum.astype(f32)
    up_sums = jnp.zeros((local_count, up_rows, model_width), f32)
    down_sums = jnp.zeros((local_count,) + down_weight.shape[1:], f32)
    for index in range(local_count):
        if index + 1 == local_count:
            last_sum, up_sums, down_sums, block_out, grad_tokens, small_sum, out_sum = (
                lax.optimization_barrier(
                    (last_sum, up_sums, down_sums, block_out, grad_tokens, small_sum, out_sum)
                )
            )
        rows = (sums[index] if index + 1 < local_count else last_sum).astype(f32)
        up_sums = lax.dynamic_update_slice(up_sums, rows[None, :up_rows], (index, 0, 0))
        down_sums = lax.dynamic_update_slice(down_sums, rows[None, up_rows:], (index, 0, 0))
    return (
        block_out[None],
        grad_tokens[None],
        small_sum[:, 0],
        qkv_sum,
        small_sum[:, 1],
        small_sum[:, 2],
        out_sum,
        small_sum[:, 3],
        small_sum[:, 4:small_count],
        up_sums,
        down_sums,
    )


def solution(mesh):
    in_specs = (
        P("fsdp", "seq", None),
        P("fsdp", "seq", None),
        P("fsdp"),
        P("fsdp", "seq", None),
        P("fsdp"),
        P("fsdp", None),
        P("fsdp"),
        P("fsdp"),
        P("fsdp", None),
        P("fsdp"),
        P("fsdp", None),
        P("seq", "fsdp", None),
        P("seq", "fsdp", None),
    )
    out_specs = (
        P("fsdp", "seq", None),
        P("fsdp", "seq", None),
        P("fsdp"),
        P("fsdp", None),
        P("fsdp"),
        P("fsdp"),
        P("fsdp", None),
        P("fsdp"),
        P("fsdp", None),
        P("seq", "fsdp", None),
        P("seq", "fsdp", None),
    )
    return jax.shard_map(local, mesh=mesh, in_specs=in_specs, out_specs=out_specs, check_vma=False)
```

```python
from functools import partial

import jax
import jax.numpy as jnp
from jax import lax
from jax.sharding import PartitionSpec as P

HEADS = 16
HEAD = 128
TOP = 8
CAP = 136


EPSILON = 1e-05
ROPE_BASE = 10000.0
NEG_FILL = -1e30


def round_up(count, unit):
    return -(-count // unit) * unit


def rms_scale(values):
    return lax.rsqrt(jnp.mean(values * values, axis=-1, keepdims=True) + EPSILON)


def norm_back(grad_rows, unit_rows, scale_rows, gain_row):
    scaled = grad_rows * gain_row
    inner = jnp.mean(scaled * unit_rows, axis=-1, keepdims=True)
    return (scale_rows * (scaled - unit_rows * inner), jnp.sum(grad_rows * unit_rows, axis=0))


def rope_tables(positions):
    half_width = HEAD // 2
    frequency = ROPE_BASE ** (-(jnp.arange(half_width, dtype=jnp.float32) * 2.0 / HEAD))
    angles = positions[:, None] * frequency[None, :]
    return (
        jnp.concatenate([jnp.cos(angles), jnp.cos(angles)], -1),
        jnp.concatenate([jnp.sin(angles), jnp.sin(angles)], -1),
    )


def rotate(values, cosine_table, sine_table):
    half_width = values.shape[-1] // 2
    turned = jnp.concatenate([-values[..., half_width:], values[..., :half_width]], -1)
    return values * cosine_table[:, None, :] + turned * sine_table[:, None, :]


def rotate_back(grad_rows, cosine_table, sine_table):
    half_width = grad_rows.shape[-1] // 2
    sine_part = grad_rows * sine_table[:, None, :]
    return grad_rows * cosine_table[:, None, :] + jnp.concatenate(
        [sine_part[..., half_width:], -sine_part[..., :half_width]], -1
    )


def from_peer(values, step):
    if step == 0:
        return values
    count = lax.axis_size("seq")
    return lax.ppermute(values, "seq", [(rank, rank ^ step) for rank in range(count)])


def gather_blocks(values):
    return jnp.stack([from_peer(values, step) for step in range(lax.axis_size("seq"))])


def return_blocks(blocks):
    return [from_peer(blocks[step], step) for step in range(lax.axis_size("seq"))]


def in_rank_order(parts):
    seq_rank = lax.axis_index("seq")
    buffer = jnp.zeros((len(parts),) + parts[0].shape, parts[0].dtype)
    for step, part in enumerate(parts):
        start = (seq_rank ^ step,) + (0,) * part.ndim
        buffer = lax.dynamic_update_slice(buffer, part[None], start)
    return buffer


def attend_block(heads_in, places, length, row_count, block_start):
    queries, keys, values = heads_in
    query_block = lax.dynamic_slice_in_dim(queries, block_start, row_count, 0)
    query_place = lax.dynamic_slice_in_dim(places, block_start, row_count, 0)
    scores = jnp.einsum(
        "qhd,khd->hqk", query_block, keys, preferred_element_type=jnp.float32
    ) * HEAD ** (-0.5)
    allowed = (places[None, :] <= query_place[:, None]) & (places[None, :] < length)
    scores = jnp.where(allowed[None], scores, NEG_FILL)
    row_max = jnp.max(scores, axis=-1, keepdims=True)
    exp_scores = jnp.exp(scores - row_max)
    denom_sum = jnp.sum(exp_scores, axis=-1, keepdims=True)
    probabilities = (exp_scores / denom_sum).astype(jnp.bfloat16)
    attended = jnp.einsum("hqk,khd->qhd", probabilities, values, preferred_element_type=jnp.float32)
    return (attended.astype(jnp.bfloat16), jnp.transpose((row_max + jnp.log(denom_sum))[..., 0]))


def attend_back(heads_in, grad_heads, log_sums, places, length, row_count, carried, block_start):
    queries, keys, values = heads_in
    grad_keys, grad_values = carried
    score_scale = HEAD ** (-0.5)
    query_block = lax.dynamic_slice_in_dim(queries, block_start, row_count, 0)
    query_place = lax.dynamic_slice_in_dim(places, block_start, row_count, 0)
    grad_block = lax.dynamic_slice_in_dim(grad_heads, block_start, row_count, 0)
    sums_block = jnp.transpose(lax.dynamic_slice_in_dim(log_sums, block_start, row_count, 0))[
        :, :, None
    ]
    scores = (
        jnp.einsum("qhd,khd->hqk", query_block, keys, preferred_element_type=jnp.float32)
        * score_scale
    )
    allowed = (places[None, :] <= query_place[:, None]) & (places[None, :] < length)
    probabilities = jnp.where(allowed[None], jnp.exp(scores - sums_block), 0.0)
    low_probs = probabilities.astype(jnp.bfloat16)
    grad_probs = jnp.einsum("qhd,khd->hqk", grad_block, values, preferred_element_type=jnp.float32)
    grad_values = grad_values + jnp.einsum(
        "hqk,qhd->khd", low_probs, grad_block, preferred_element_type=jnp.float32
    )
    inner = jnp.sum(probabilities * grad_probs, axis=-1, keepdims=True)
    grad_scores = (probabilities * (grad_probs - inner)).astype(jnp.bfloat16)
    grad_query = (
        jnp.einsum("hqk,khd->qhd", grad_scores, keys, preferred_element_type=jnp.float32)
        * score_scale
    )
    grad_keys = (
        grad_keys
        + jnp.einsum("hqk,qhd->khd", grad_scores, query_block, preferred_element_type=jnp.float32)
        * score_scale
    )
    return ((grad_keys, grad_values), grad_query)


def mixed_dot(form, left, right):
    return jnp.einsum(form, left, right, preferred_element_type=jnp.float32)


def expert_forward(rows, grad_result_rows, slot_weight, gate_up, down):
    half_width = down.shape[0]
    gate_up_out = mixed_dot("rd,df->rf", rows, gate_up)
    gate_part = gate_up_out[:, :half_width]
    up_part = gate_up_out[:, half_width:]
    sigmoid_gate = jax.nn.sigmoid(gate_part)
    hidden = (gate_part * sigmoid_gate * up_part).astype(jnp.bfloat16)
    grad_result = (grad_result_rows.astype(jnp.float32) * slot_weight[:, None]).astype(jnp.bfloat16)
    grad_hidden = mixed_dot("rd,fd->rf", grad_result, down)
    grad_gate = grad_hidden * up_part * sigmoid_gate * (1.0 + gate_part * (1.0 - sigmoid_gate))
    grad_up = grad_hidden * gate_part * sigmoid_gate
    grad_mixed = jnp.concatenate([grad_gate, grad_up], -1).astype(jnp.bfloat16)
    grad_rows = mixed_dot("rd,fd->rf", grad_mixed, gate_up).astype(jnp.bfloat16)
    result = mixed_dot("rf,fd->rd", hidden, down).astype(jnp.bfloat16)
    grad_slot = jnp.sum(
        result.astype(jnp.float32) * grad_result_rows.astype(jnp.float32), axis=-1
    )
    weighted = (result.astype(jnp.float32) * slot_weight[:, None]).astype(jnp.bfloat16)
    return (weighted, grad_slot, grad_rows, (rows, grad_mixed, hidden, grad_result))


def expert_weights(kept):
    rows, grad_mixed, hidden, grad_result = kept
    grad_gate_up = mixed_dot("rd,rf->df", rows, grad_mixed).astype(jnp.bfloat16)
    grad_down = mixed_dot("rf,rd->fd", hidden, grad_result).astype(jnp.bfloat16)
    return (grad_gate_up, grad_down)


def after(values, *earlier):
    return lax.optimization_barrier((values, earlier))[0]


def split_rows(stacked, up_rows):
    count = lax.axis_size("fsdp")
    width = stacked.shape[-1]
    stacked = stacked.reshape(count, -1, width)
    return (stacked[:, :up_rows].reshape(-1, width), stacked[:, up_rows:].reshape(-1, width))


def chip_sums(*grads):
    count = lax.axis_size("fsdp")
    core = lax.axis_index("fsdp") % 2
    width = grads[0].shape[-1]
    parts = [grad.reshape(count // 2, 2, -1, width) for grad in grads]

    def side(number):
        return jnp.concatenate(
            [lax.dynamic_index_in_dim(part, number, 1, False) for part in parts], axis=1
        )

    swapped = lax.ppermute(side(1 - core), "fsdp", [(index, index ^ 1) for index in range(count)])
    total = side(core).astype(jnp.float32) + swapped.astype(jnp.float32)
    return total.astype(grads[0].dtype).reshape(-1, width)


def scatter_chips(rows):
    count = lax.axis_size("fsdp")
    groups = [list(range(core, count, 2)) for core in range(2)]
    return lax.psum_scatter(
        rows, "fsdp", scatter_dimension=0, tiled=True, axis_index_groups=groups
    )


def local(
    tokens,
    cotangent,
    lengths,
    experts,
    attn_gain,
    qkv_weight,
    q_gain,
    k_gain,
    out_weight,
    moe_gain,
    router_weight,
    gate_up_weight,
    down_weight,
):
    bf16, f32 = jnp.bfloat16, jnp.float32
    seq_count = lax.axis_size("seq")
    seq_rank = lax.axis_index("seq")
    own_tokens = tokens[0]
    tok_count, model_width = own_tokens.shape
    local_count = gate_up_weight.shape[0]
    experts_count = local_count * seq_count
    own_width = model_width // seq_count
    own_heads = own_width // HEAD
    key_span = seq_count * tok_count
    length = lengths[0]
    block_ranks = seq_rank ^ jnp.arange(seq_count, dtype=jnp.int32)
    places = (
        block_ranks[:, None] * tok_count + jnp.arange(tok_count, dtype=jnp.int32)[None, :]
    ).reshape(-1)
    valid_all = (places < length).reshape(seq_count, tok_count)
    keep_mask = valid_all[0].astype(f32)[:, None]
    up_rows = gate_up_weight.shape[1]
    shards = [
        jnp.concatenate([gate_up_weight[index], down_weight[index]], axis=0)
        for index in range(local_count)
    ]

    own_qkv = [
        lax.dynamic_slice_in_dim(
            qkv_weight, kind * model_width + seq_rank * own_width, own_width, 1
        )
        for kind in range(3)
    ]
    own_small = jnp.concatenate(
        [jnp.stack([attn_gain, q_gain, k_gain, moe_gain], axis=1), router_weight], axis=1
    )
    small_count = 4 + experts_count
    small_width = round_up(small_count, 32)
    own_small = jnp.pad(own_small, ((0, 0), (0, small_width - small_count)))
    front = jnp.concatenate(own_qkv + [own_small], axis=1)
    front_full = lax.all_gather(front, "fsdp", axis=0, tiled=True)
    token_blocks = gather_blocks(own_tokens)
    out_cut = lax.dynamic_slice_in_dim(out_weight, seq_rank * own_width, own_width, 1)
    out_cut = lax.all_gather(after(out_cut, front), "fsdp", axis=0, tiled=True)
    gather_expert = lambda index, *earlier: lax.all_gather(
        after(shards[index], *earlier), "fsdp", axis=0, tiled=True
    )
    weights = [gather_expert(0, front_full)]
    id_rows = experts[0].astype(bf16).reshape(-1, model_width)
    cot_rows = after(jnp.concatenate([cotangent[0], id_rows], axis=0), token_blocks)
    cot_parts = [from_peer(cot_rows, step) for step in range(min(3, seq_count))]

    qkv_own = front_full[:, : 3 * own_width]
    small_full = front_full[:, 3 * own_width : 3 * own_width + small_count].T
    gain_one, gain_q, gain_k, gain_two = [small_full[i].astype(f32) for i in range(4)]
    router_rows = small_full[4:]
    gain_q = lax.dynamic_slice_in_dim(gain_q, seq_rank * own_width, own_width, 0)
    gain_k = lax.dynamic_slice_in_dim(gain_k, seq_rank * own_width, own_width, 0)
    inputs_all = token_blocks.reshape(key_span, model_width).astype(f32)
    scale_all = rms_scale(inputs_all)
    normed = (inputs_all * scale_all * gain_one).astype(bf16)
    projected = mixed_dot("td,de->te", normed, qkv_own)
    query_raw = projected[:, :own_width]
    key_raw = projected[:, own_width : 2 * own_width]
    value_raw = projected[:, 2 * own_width :]
    squares = jnp.stack([jnp.sum(query_raw * query_raw, -1), jnp.sum(key_raw * key_raw, -1)])

    def over_heads(parts):
        blocks = parts.reshape(2, seq_count, tok_count)
        total = blocks
        for step in range(1, seq_count):
            order = jnp.array([block ^ step for block in range(seq_count)])
            total = total + from_peer(blocks, step)[:, order]
        return total.reshape(2, key_span)

    scales = lax.rsqrt(over_heads(squares) / model_width + EPSILON)[:, :, None]
    unit_q = query_raw * scales[0]
    unit_k = key_raw * scales[1]
    cosine_table, sine_table = rope_tables(places.astype(f32))
    head_shape = (key_span, own_heads, HEAD)
    query_rot = rotate((unit_q * gain_q).reshape(head_shape), cosine_table, sine_table)
    key_rot = rotate((unit_k * gain_k).reshape(head_shape), cosine_table, sine_table)
    heads_in = (
        query_rot.astype(bf16),
        key_rot.astype(bf16),
        value_raw.reshape(head_shape).astype(bf16),
    )

    row_count = min(512, key_span)
    block_starts = jnp.arange(key_span // row_count, dtype=jnp.int32) * row_count
    attended_blocks, sums_blocks = lax.map(
        partial(attend_block, heads_in, places, length, row_count), block_starts
    )
    log_sums = sums_blocks.reshape(key_span, own_heads)
    weights.append(gather_expert(1, heads_in))
    cot_parts += [from_peer(after(cot_rows, heads_in), step) for step in range(3, seq_count)]
    cot_parts = jnp.stack(cot_parts)
    cot_blocks = cot_parts[:, :tok_count]
    id_blocks = cot_parts[:, tok_count:].reshape(seq_count, tok_count, -1).astype(jnp.int32)
    out_cut = after(out_cut, heads_in)
    out_parts = [from_peer(out_cut, step) for step in range(seq_count)]

    out_full = in_rank_order(out_parts)
    attended_parts = return_blocks(attended_blocks.reshape(seq_count, tok_count, own_width))
    attended = jnp.transpose(in_rank_order(attended_parts), (1, 0, 2))
    inputs = own_tokens.astype(f32)
    branch = mixed_dot(
        "td,jdc->tjc", attended.reshape(tok_count, model_width), out_full
    ).reshape(tok_count, model_width)
    middle = inputs + branch * keep_mask
    scale_two = rms_scale(middle)
    unit_two = middle * scale_two
    normed_two = (unit_two * gain_two).astype(bf16)

    row_blocks = gather_blocks(normed_two)
    weights.append(gather_expert(2, normed_two))
    weights += [gather_expert(index, row_blocks) for index in range(3, local_count)]
    logits = mixed_dot("btd,ed->bte", row_blocks, router_rows)
    expert_range = jnp.arange(experts_count, dtype=jnp.int32)
    named = jnp.any(id_blocks[..., None] == expert_range, axis=2)
    chosen = jnp.where(named, logits, NEG_FILL)
    exp_chosen = jnp.where(named, jnp.exp(chosen - jnp.max(chosen, -1, keepdims=True)), 0.0)
    gates = exp_chosen / jnp.sum(exp_chosen, axis=-1, keepdims=True)
    routed = (named & valid_all[..., None]).astype(jnp.int32)
    before = jnp.cumsum(routed, axis=1) - routed
    local_routed = lax.dynamic_slice_in_dim(routed, seq_rank * local_count, local_count, 2)
    local_before = lax.dynamic_slice_in_dim(before, seq_rank * local_count, local_count, 2)
    local_gates = lax.dynamic_slice_in_dim(gates, seq_rank * local_count, local_count, 2)
    slot_count = round_up(CAP, 16)
    slot_place = jnp.where(local_routed == 1, local_before, -1)
    slot_place = jnp.transpose(slot_place, (2, 0, 1))
    local_gates = jnp.transpose(local_gates, (2, 0, 1))
    slot_hit = slot_place[:, :, None, :] == jnp.arange(slot_count, dtype=jnp.int32)[:, None]
    slot_pick = slot_hit.astype(bf16)
    slot_gates = jnp.sum(jnp.where(slot_hit, local_gates[:, :, None, :], 0.0), axis=-1)

    def picked(index):
        return tuple(
            mixed_dot("bct,btd->bcd", slot_pick[index], blocks)
            .astype(bf16)
            .reshape(seq_count * slot_count, model_width)
            for blocks in (row_blocks, cot_blocks)
        )

    def computed(index, pair):
        weighted, grad_slot, grad_rows, kept = expert_forward(
            *pair, slot_gates[index].reshape(-1), *split_rows(weights[index], up_rows)
        )
        weighted_rows.append(weighted.reshape(seq_count, slot_count, model_width))
        grad_row_sets.append(grad_rows.reshape(seq_count, slot_count, model_width))
        grad_slots.append(
            jnp.sum(
                jnp.where(
                    slot_hit[index], grad_slot.reshape(seq_count, slot_count)[:, :, None], 0.0
                ),
                1,
            )
        )
        return kept

    weighted_rows, grad_row_sets, grad_slots, sums = [], [], [], []
    scatter = lambda grads: lax.psum_scatter(grads, "fsdp", scatter_dimension=0, tiled=True)
    pair = picked(0)
    for index in range(local_count):
        kept = computed(index, pair)
        if index + 1 < local_count:
            grads = chip_sums(*expert_weights(kept))
            pair = after(picked(index + 1), grads)
            if index + 2 < local_count:
                sums.append(scatter_chips(grads))
    pick_all = jnp.concatenate([slot_pick[index] for index in range(local_count)], axis=1)
    grad_partial = mixed_dot("bct,bcd->btd", pick_all, jnp.concatenate(grad_row_sets, axis=1))

    grad_gates = return_blocks(jnp.stack(grad_slots, axis=1))
    grad_back = return_blocks(grad_partial.astype(bf16))
    moe_partial = mixed_dot("bct,bcd->btd", pick_all, jnp.concatenate(weighted_rows, axis=1))
    last_grads = expert_weights(kept)
    grad_back = after(grad_back, last_grads, moe_partial.astype(bf16))

    own_gates = gates[0]
    grad_gates = jnp.transpose(in_rank_order(grad_gates), (2, 0, 1)).reshape(
        tok_count, experts_count
    )
    grad_logits = own_gates * (
        grad_gates - jnp.sum(own_gates * grad_gates, axis=-1, keepdims=True)
    )
    grad_out = cotangent[0].astype(f32) * keep_mask
    grad_normed_two = jnp.einsum(
        "te,ed->td", grad_logits, router_rows.astype(f32), precision=lax.Precision.HIGHEST
    ) + sum(part.astype(f32) for part in grad_back)
    grad_router = jnp.einsum(
        "te,td->ed", grad_logits, normed_two.astype(f32), precision=lax.Precision.HIGHEST
    )
    grad_middle_norm, grad_two = norm_back(grad_normed_two, unit_two, scale_two, gain_two)
    grad_middle = grad_out + grad_middle_norm
    grad_branch = (grad_middle * keep_mask).astype(bf16)
    grad_attended = mixed_dot(
        "tjc,jdc->td", grad_branch.reshape(tok_count, seq_count, own_width), out_full
    ).astype(bf16)
    cut_heads = grad_attended.reshape(tok_count, seq_count, own_width)
    grad_heads = jnp.stack(
        [
            from_peer(lax.dynamic_index_in_dim(cut_heads, seq_rank ^ step, 1, False), step)
            for step in range(seq_count)
        ]
    ).reshape(head_shape)

    sums.append(scatter_chips(after(grads, grad_heads, *sums[:1])))
    moe_parts = return_blocks(after(moe_partial.astype(bf16), grad_heads))
    zero_heads = jnp.zeros(head_shape, f32)
    (grad_keys, grad_values), grad_queries = lax.scan(
        partial(attend_back, heads_in, grad_heads, log_sums, places, length, row_count),
        (zero_heads, zero_heads),
        block_starts,
    )

    grad_queries = after(grad_queries, moe_parts)
    low = lambda rows: rows.reshape(head_shape).astype(bf16).astype(f32)
    grad_qn = rotate_back(low(grad_queries), cosine_table, sine_table).reshape(key_span, own_width)
    grad_kn = rotate_back(low(grad_keys), cosine_table, sine_table).reshape(key_span, own_width)
    scaled_q = grad_qn * gain_q
    scaled_k = grad_kn * gain_k
    inners = over_heads(
        jnp.stack([jnp.sum(scaled_q * unit_q, -1), jnp.sum(scaled_k * unit_k, -1)])
    )
    grad_branch = after(grad_branch, inners)
    grad_cut = mixed_dot("td,tc->dc", attended.reshape(tok_count, model_width), grad_branch)
    grad_cut = grad_cut.astype(bf16).reshape(model_width, seq_count, own_width)
    grad_cut = [
        lax.dynamic_index_in_dim(grad_cut, seq_rank ^ step, 1, False) for step in range(seq_count)
    ]
    near_cuts = [from_peer(grad_cut[step], step) for step in range(min(3, seq_count))]
    far_cuts = [
        from_peer(after(grad_cut[step], near_cuts), step) for step in range(3, seq_count)
    ]
    inners = (inners / model_width)[:, :, None]
    grad_projected = jnp.concatenate(
        [
            scales[0] * (scaled_q - unit_q * inners[0]),
            scales[1] * (scaled_k - unit_k * inners[1]),
            grad_values.reshape(key_span, own_width),
        ],
        axis=1,
    ).astype(bf16)
    grad_normed = mixed_dot("te,de->td", grad_projected, qkv_own)
    grad_one = jnp.sum(grad_normed * (inputs_all * scale_all), axis=0)
    grad_qkv = mixed_dot("td,te->de", normed, grad_projected).astype(bf16)
    placed = lambda row: lax.dynamic_update_slice(
        jnp.zeros((model_width,), f32), row, (seq_rank * own_width,)
    )
    grad_small = jnp.concatenate(
        [
            jnp.stack(
                [
                    grad_one,
                    placed(jnp.sum(grad_qn * unit_q, axis=0)),
                    placed(jnp.sum(grad_kn * unit_k, axis=0)),
                    grad_two,
                ]
            ),
            grad_router,
            jnp.zeros((small_width - small_count, model_width), f32),
        ],
        axis=0,
    )
    grad_front = jnp.concatenate([grad_qkv, grad_small.T.astype(bf16)], axis=1)
    grad_front = after(grad_front, near_cuts)

    front_sum = scatter_chips(after(chip_sums(grad_front), *sums[:-1]))
    grad_cut = sum(part.astype(f32) for part in near_cuts + far_cuts).astype(bf16)
    out_sum = scatter(after(grad_cut, *sums, grad_front))
    last_grads = chip_sums(*after(last_grads, grad_front))
    grad_normed = return_blocks(grad_normed.astype(bf16).reshape(seq_count, tok_count, model_width))
    front_parts = [from_peer(front_sum, step) for step in range(seq_count)]
    block_out = (middle + sum(part.astype(f32) for part in moe_parts)).astype(bf16)
    grad_normed = sum(part.astype(f32) for part in grad_normed)
    scale_one = rms_scale(inputs)
    scaled = grad_normed * gain_one
    unit_one = inputs * scale_one
    inner = jnp.mean(scaled * unit_one, axis=-1, keepdims=True)
    grad_tokens = (grad_middle + scale_one * (scaled - unit_one * inner)).astype(bf16)
    small_sum = sum(part[:, 3 * own_width :].astype(f32) for part in front_parts)
    qkv_sum = in_rank_order([part[:, : 3 * own_width] for part in front_parts])
    qkv_sum = jnp.transpose(
        qkv_sum.reshape(seq_count, -1, 3, own_width), (1, 2, 0, 3)
    ).reshape(-1, 3 * model_width)
    out_sum = in_rank_order([from_peer(out_sum, step) for step in range(seq_count)])
    out_sum = jnp.transpose(out_sum, (1, 0, 2)).reshape(-1, model_width)
    last_sum = scatter_chips(after(last_grads, front_sum))
    qkv_sum, out_sum = qkv_sum.astype(f32), out_sum.astype(f32)
    up_sums = jnp.zeros((local_count, up_rows, model_width), f32)
    down_sums = jnp.zeros((local_count,) + down_weight.shape[1:], f32)
    for index in range(local_count):
        if index + 1 == local_count:
            last_sum, up_sums, down_sums, block_out, grad_tokens, small_sum, out_sum = (
                lax.optimization_barrier(
                    (last_sum, up_sums, down_sums, block_out, grad_tokens, small_sum, out_sum)
                )
            )
        rows = (sums[index] if index + 1 < local_count else last_sum).astype(f32)
        up_sums = lax.dynamic_update_slice(up_sums, rows[None, :up_rows], (index, 0, 0))
        down_sums = lax.dynamic_update_slice(down_sums, rows[None, up_rows:], (index, 0, 0))
    return (
        block_out[None],
        grad_tokens[None],
        small_sum[:, 0],
        qkv_sum,
        small_sum[:, 1],
        small_sum[:, 2],
        out_sum,
        small_sum[:, 3],
        small_sum[:, 4:small_count],
        up_sums,
        down_sums,
    )


def solution(mesh):
    in_specs = (
        P("fsdp", "seq", None),
        P("fsdp", "seq", None),
        P("fsdp"),
        P("fsdp", "seq", None),
        P("fsdp"),
        P("fsdp", None),
        P("fsdp"),
        P("fsdp"),
        P("fsdp", None),
        P("fsdp"),
        P("fsdp", None),
        P("seq", "fsdp", None),
        P("seq", "fsdp", None),
    )
    out_specs = (
        P("fsdp", "seq", None),
        P("fsdp", "seq", None),
        P("fsdp"),
        P("fsdp", None),
        P("fsdp"),
        P("fsdp"),
        P("fsdp", None),
        P("fsdp"),
        P("fsdp", None),
        P("seq", "fsdp", None),
        P("seq", "fsdp", None),
    )
    return jax.shard_map(local, mesh=mesh, in_specs=in_specs, out_specs=out_specs, check_vma=False)
```
